32 devices in a mesh: grp: 2 (over x), blk: 8 (over z, y), node: 2 (over core).
Axes of the slice: x: 2, y: 2, z: 4, core: 2. Of those that a mesh axis runs over, the one named last changes fastest.
Arguments:
- queries: bfloat16 [32768, 128], P(('grp', 'blk', 'node')), parts along dimension 0, may hold values from -24 to 24
- keys: bfloat16 [32768, 128], P(('grp', 'blk', 'node')), parts along dimension 0, may hold values from -24 to 24
- values: bfloat16 [32768, 128], P(('grp', 'blk', 'node')), parts along dimension 0, may hold values from -6 to 6
- allowed: int32 [256, 128], P('grp'), parts along dimension 0, may hold values from 0 to 1, as said below
Outputs:
- attended: bfloat16 [32768, 128], P(('grp', 'blk', 'node')), parts along dimension 0
The draws below stay inside these ranges and needn't reach their ends.
There are 2 independent parts, one for each index of `grp`. The reference program is written for one: setup_inputs(seed, part) draws one part's arguments, and reference() takes and returns one part's arrays. A program takes and returns all parts, laid end to end along the dimension named above; each array names one. Nothing has to cross between parts.
Inputs may be any that keep to these rules, and one draw needn't show every extreme that they name: allowed[i, i] is 1. allowed[i, j] is 0 where token blocks i and j lie in pairs of 2048 tokens (index // 16) more than 3 apart; in every draw some allowed entries lie exactly 3 pairs apart. Within that range it thins with the frame distance of the blocks.
All inputs are finite; a program needn't handle non-finite values.
Results may differ from the reference program's by a relative error of at most 0.007.
Values may be sent and summed in bfloat16 or wider, within the bound.
No kernel may reach another device: no remote copies, remote signals or barrier semaphores. Data moves between devices by JAX's collectives and lax.ppermute only.
A program may use at most 192 MiB of HBM per device.

```python
import jax
import jax.numpy as jnp
from jax import lax

HEAD = 128
HEADS = 1
BLOCK = 128
FRAME_BLK = 2
REACH = 3
TOK_DEV = 1024
SEQ = 16384
NB = 128
N_NODE = 2


def shared_pair(key):
    width = HEADS * HEAD
    base_query = jnp.clip(jax.random.normal(jax.random.fold_in(key, 11), (SEQ, width), jnp.float32), -5.0, 5.0)
    base_key = jnp.clip(jax.random.normal(jax.random.fold_in(key, 12), (SEQ, width), jnp.float32), -5.0, 5.0)
    return (base_query, base_key)


def draw_queries(key, part):
    return shared_pair(key)[0].astype(jnp.bfloat16)


def draw_keys(key, part):
    return shared_pair(key)[1].astype(jnp.bfloat16)


def draw_allowed(key, part):
    pair_blocks = TOK_DEV * N_NODE // BLOCK
    first = jnp.arange(NB)[:, None]
    second = jnp.arange(NB)[None, :]
    near = jnp.abs(first // pair_blocks - second // pair_blocks) <= REACH
    distance = jnp.abs(first // FRAME_BLK - second // FRAME_BLK)
    rolled = jax.random.randint(key, (NB, NB), 0, 1 << 20)
    keep = (distance <= 1) | (rolled % jnp.maximum(distance, 1) == 0)
    edge = jnp.abs(first - second) == REACH * pair_blocks
    return jnp.where(near & (keep | edge), 1, 0).astype(jnp.int32)


def level_of(key, shape, pieces, low, largest):
    def one(position, blocks):
        steps = jax.random.uniform(jax.random.fold_in(jax.random.fold_in(key, 6), position), (blocks,), jnp.float32, low / len(pieces), largest / len(pieces))
        return jnp.repeat(jnp.exp(steps), shape[position] // blocks).reshape((-1,) + (1,) * (len(shape) - position - 1))

    gain = one(*pieces[0])
    for cut in pieces[1:]:
        gain = gain * one(*cut)
    return gain


def noise(own_key, shape, scale, limit, split=(), kind=jnp.bfloat16):
    values = jax.random.normal(own_key, shape, jnp.float32) * scale
    if len(split) > 0:
        values = level_of(own_key, shape, split, -0.22, 0.18) * values
    return jnp.clip(values, min=-limit, max=limit).astype(kind)


def setup_inputs(seed: int = 0, part: int = 0) -> dict:
    key_of = jax.random.split(jax.random.key(seed), 5)
    part_keys = jax.random.split(jax.random.fold_in(key_of[4], part), 5)
    queries = draw_queries(jax.random.fold_in(jax.random.fold_in(key_of[4], part), 71), part)
    keys = draw_keys(jax.random.fold_in(jax.random.fold_in(key_of[4], part), 71), part)
    values = noise(part_keys[2], (SEQ, HEADS * HEAD), 1.0, 6.0, ((0, 16),))
    allowed = draw_allowed(jax.random.fold_in(jax.random.fold_in(key_of[4], part), 71), part)
    return dict(queries=queries, keys=keys, values=values, allowed=allowed)


def reference(queries, keys, values, allowed):
    pair = TOK_DEV * N_NODE
    pairs = SEQ // pair
    pad_rows = REACH * pair
    width = (2 * REACH + 1) * pair
    pair_blocks = pair // BLOCK
    width_blocks = width // BLOCK
    scale = HEAD ** -0.5
    key_pad = jnp.pad(keys, ((pad_rows, pad_rows), (0, 0)))
    value_pad = jnp.pad(values, ((pad_rows, pad_rows), (0, 0)))
    mask_pad = jnp.pad(allowed, ((0, 0), (pad_rows // BLOCK, pad_rows // BLOCK)))

    def one_pair(index):
        start = (index * pair).astype(jnp.int32)
        block_start = (index * pair_blocks).astype(jnp.int32)
        query_rows = lax.dynamic_slice_in_dim(queries, start, pair, 0).reshape(pair, HEADS, HEAD)
        key_rows = lax.dynamic_slice_in_dim(key_pad, start, width, 0).reshape(width, HEADS, HEAD)
        value_rows = lax.dynamic_slice_in_dim(value_pad, start, width, 0).reshape(width, HEADS, HEAD)
        tile = lax.dynamic_slice(mask_pad, (block_start, block_start), (pair_blocks, width_blocks)) > 0
        mask = jnp.broadcast_to(tile[:, None, :, None], (pair_blocks, BLOCK, width_blocks, BLOCK)).reshape(pair, width)
        score = jnp.einsum('qhd,khd->hqk', query_rows.astype(jnp.float32), key_rows.astype(jnp.float32)) * scale
        score = jnp.where(mask[None], score, -1e30)
        top = jnp.max(score, axis=-1, keepdims=True)
        weight = jnp.where(mask[None], jnp.exp(score - top), 0.0)
        total = jnp.sum(weight, axis=-1)
        rounded = lax.optimization_barrier(weight.astype(jnp.bfloat16))
        summed = jnp.einsum('hqk,khd->hqd', rounded.astype(jnp.float32), value_rows.astype(jnp.float32))
        result = summed / total[..., None]
        return jnp.transpose(result, (1, 0, 2)).reshape(pair, HEADS * HEAD).astype(jnp.bfloat16)

    stacked = lax.map(one_pair, jnp.arange(pairs, dtype=jnp.int32))
    return stacked.reshape(SEQ, HEADS * HEAD)
```

```python
import functools
import math

import jax
import jax.numpy as jnp
from jax import lax
from jax.experimental import pallas as pl
from jax.experimental.pallas import tpu as pltpu
from jax.sharding import PartitionSpec as P

HEAD = 128
BLOCK = 128
FLOOR = -1e30
DROP = -3e38
FACTOR = HEAD ** (-0.5) * math.log2(math.e)
COUNT_AT = 64
STATS = 48

ANY = pl.BlockSpec(memory_space=pl.ANY)
VMEM = pl.BlockSpec(memory_space=pltpu.VMEM)
SMEM = pl.BlockSpec(memory_space=pltpu.SMEM)


def cost(flops, moved, exps=0):
    return pl.CostEstimate(flops=flops, bytes_accessed=moved, transcendentals=exps)


def bundle_kernel(k_ref, v_ref, out_ref):
    out_ref[0] = k_ref[...]
    for block in range(v_ref.shape[0] // BLOCK):
        at = pl.ds(block * BLOCK, BLOCK)
        out_ref[1, at, :] = v_ref[at, :].T


def bundle(keys, values):
    rows = keys.shape[0]
    return pl.pallas_call(
        bundle_kernel,
        out_shape=jax.ShapeDtypeStruct((2, rows, HEAD), keys.dtype),
        in_specs=[VMEM, VMEM],
        out_specs=VMEM,
        cost_estimate=cost(0, 4 * rows * HEAD * 2),
        name="bundle",
    )(keys, values)


def list_kernel(spots, allowed_ref, out_ref, rows_ref, sems):
    own = out_ref.shape[0] // 5
    pos = lax.axis_index("blk")
    core = lax.axis_index("node")
    side = pos % 2
    high = pos // 2
    levels = spots // 2
    mate = pos + 1 - 2 * side
    extra = pos - 1 + 2 * side
    extra_ok = (extra >= 0) & (extra < spots)
    first = high + 1 - 2 * (high % 2)
    second = high - 1 + 2 * (high % 2)
    first_ok = (first >= 0) & (first < levels)
    second_ok = (second >= 0) & (second < levels)
    far = high + 1 - 2 * side
    pair = 2 * own
    query_pairs = (pos, mate, jnp.where(extra_ok, extra, 0))
    copies = []
    for group, who in enumerate(query_pairs):
        begin = pl.multiple_of(who * pair + core * own, own)
        copies.append(
            pltpu.make_async_copy(
                allowed_ref.at[pl.ds(begin, own), :], rows_ref.at[group], sems.at[group]
            )
        )
    for copy in copies:
        copy.start()
    for copy in copies:
        copy.wait()

    def halves(who, ok):
        base = jnp.where(ok, who * pair, 0)
        ok = ok.astype(jnp.int32)
        return [(base + core * own, ok), (base + (1 - core) * own, ok)]

    near = halves(pos, pos >= 0)
    one = halves(first * 2 + side, first_ok)
    two = halves(second * 2 + side, second_ok)
    beside = one + two
    one_x = halves(first * 2 + side, first_ok & extra_ok & (first == far))
    two_x = halves(second * 2 + side, second_ok & extra_ok & (second == far))
    jobs = ((0, near), (1, near), (1, beside), (0, beside), (2, one_x + two_x))
    for job, (group, parts) in enumerate(jobs):

        def row(i, carry, job=job, group=group, parts=parts):
            count = jnp.int32(0)
            for part, (start, ok) in enumerate(parts):
                for j in range(own):
                    out_ref[job * own + i, count] = jnp.int32(part * own + j)
                    kept = (rows_ref[group, i, start + j] > 0).astype(jnp.int32)
                    count = count + kept * ok
            out_ref[job * own + i, COUNT_AT] = count
            return carry

        lax.fori_loop(0, own, row, 0)


def lists(allowed, own, spots):
    return pl.pallas_call(
        functools.partial(list_kernel, spots),
        out_shape=jax.ShapeDtypeStruct((5 * own, 128), jnp.int32),
        in_specs=[ANY],
        out_specs=SMEM,
        scratch_shapes=[
            pltpu.SMEM((3, own, allowed.shape[1]), jnp.int32),
            pltpu.SemaphoreType.DMA((3,)),
        ],
        cost_estimate=cost(1000, 100000),
        name="lists",
    )(allowed)


def thirds(value):
    high = value.astype(jnp.bfloat16)
    rest = value - high.astype(jnp.float32)
    middle = rest.astype(jnp.bfloat16)
    low = (rest - middle.astype(jnp.float32)).astype(jnp.bfloat16)
    return high, middle, low


def attend_kernel(job, sources, resume, pack, list_ref, q_ref, *refs):
    source_refs = refs[:sources]
    refs = refs[sources:]
    own = q_ref.shape[0] // BLOCK
    rows = q_ref.shape[0]
    if resume:
        sum_in, stat_in = refs[:2]
        refs = refs[2:]
    if pack:
        packed_ref, sum_ref, k_ref, v_ref, sems = refs
    else:
        sum_ref, stat_ref, k_ref, v_ref, sems = refs
    copies = []
    for n, ref in enumerate(source_refs):
        at = pl.ds(n * rows, rows)
        copies.append(pltpu.make_async_copy(ref.at[0], k_ref.at[at, :], sems.at[2 * n]))
        copies.append(pltpu.make_async_copy(ref.at[1], v_ref.at[at, :], sems.at[2 * n + 1]))
    for copy in copies:
        copy.start()
    counts = [list_ref[job * own + i, COUNT_AT] for i in range(own)]
    steps = counts[0]
    for count in counts[1:]:
        steps = jnp.maximum(steps, count)
    if resume:
        sum_ref[...] = sum_in[...]
        tops = tuple(stat_in[pl.ds(i, 1), :] for i in range(own))
        totals = tuple(stat_in[pl.ds(own + i, 1), :] for i in range(own))
    else:
        sum_ref[...] = jnp.zeros_like(sum_ref)
        tops = tuple(jnp.full((1, BLOCK), FLOOR, jnp.float32) for _ in range(own))
        totals = tuple(jnp.zeros((1, BLOCK), jnp.float32) for _ in range(own))
    for copy in copies:
        copy.wait()

    def step(t, state):
        tops, totals = state
        new_tops, new_totals = [], []
        for i in range(own):
            live = t < counts[i]
            index = jnp.where(live, list_ref[job * own + i, t], 0)
            bias = jnp.where(live, jnp.float32(0.0), jnp.float32(DROP))
            at = pl.ds(pl.multiple_of(index * BLOCK, BLOCK), BLOCK)
            mine = pl.ds(i * BLOCK, BLOCK)
            score = lax.dot_general(
                k_ref[at, :],
                q_ref[mine, :],
                (((1,), (1,)), ((), ())),
                preferred_element_type=jnp.float32,
            )
            top = jnp.maximum(tops[i], jnp.max(score, axis=0, keepdims=True) + bias)
            weight = jnp.exp2((score + (bias - top)) * FACTOR)
            fade = jnp.exp2((tops[i] - top) * FACTOR)
            new_totals.append(totals[i] * fade + jnp.sum(weight, axis=0, keepdims=True))
            new_tops.append(top)
            part = lax.dot_general(
                v_ref[at, :],
                weight.astype(jnp.bfloat16),
                (((1,), (0,)), ((), ())),
                preferred_element_type=jnp.float32,
            )
            sum_ref[mine, :] = sum_ref[mine, :] * fade + part
        return tuple(new_tops), tuple(new_totals)

    tops, totals = lax.fori_loop(0, steps, step, (tops, totals))
    if pack:
        for i in range(own):
            mine = pl.ds(i * BLOCK, BLOCK)
            inverse = 1.0 / jnp.maximum(totals[i], 1e-30)
            packed_ref[mine, :] = (sum_ref[mine, :] * inverse).astype(jnp.bfloat16)
        pieces = thirds(jnp.concatenate(tops + totals, axis=0))
        for n, piece in enumerate(pieces):
            packed_ref[pl.ds(rows + n * 2 * own, 2 * own), :] = piece
    else:
        stat_ref[...] = jnp.concatenate(tops + totals, axis=0)


def attend(job, table, queries, sources, state=None, pack=False):
    rows = queries.shape[0]
    own = rows // BLOCK
    keys = len(sources) * rows
    resume = state is not None
    sums = jax.ShapeDtypeStruct((rows, HEAD), jnp.float32)
    if pack:
        out_shape = jax.ShapeDtypeStruct((rows + 6 * own, HEAD), jnp.bfloat16)
        out_specs = VMEM
        scratch = [pltpu.VMEM((rows, HEAD), jnp.float32)]
    else:
        out_shape = (sums, jax.ShapeDtypeStruct((2 * own, BLOCK), jnp.float32))
        out_specs = (VMEM, VMEM)
        scratch = []
    scratch += [
        pltpu.VMEM((keys, HEAD), jnp.bfloat16),
        pltpu.VMEM((keys, HEAD), jnp.bfloat16),
        pltpu.SemaphoreType.DMA((2 * len(sources),)),
    ]
    extra = list(state) if resume else []
    return pl.pallas_call(
        functools.partial(attend_kernel, job, len(sources), resume, pack),
        out_shape=out_shape,
        in_specs=[SMEM, VMEM] + [ANY] * len(sources) + [VMEM] * len(extra),
        out_specs=out_specs,
        scratch_shapes=scratch,
        cost_estimate=cost(rows * keys * HEAD, 4 * keys * HEAD, rows * keys // 4),
        compiler_params=pltpu.CompilerParams(vmem_limit_bytes=24 << 20),
        name="attend%d" % job,
    )(table, queries, *sources, *extra)


def merge_kernel(sum_ref, stat_ref, one_ref, two_ref, out_ref):
    rows = sum_ref.shape[0]
    own = rows // BLOCK

    def stats(ref):
        pieces = [
            ref[pl.ds(rows + n * 2 * own, 2 * own), :].astype(jnp.float32) for n in range(3)
        ]
        both = (pieces[2] + pieces[1]) + pieces[0]
        top, total = both[:own], both[own:]
        return jnp.where(total > 0, top, FLOOR), total

    top0, total0 = stat_ref[pl.ds(0, own), :], stat_ref[pl.ds(own, own), :]
    top1, total1 = stats(one_ref)
    top2, total2 = stats(two_ref)
    top = jnp.maximum(jnp.maximum(top0, top1), top2)
    part0 = jnp.exp2((top0 - top) * FACTOR)
    part1 = jnp.exp2((top1 - top) * FACTOR) * total1
    part2 = jnp.exp2((top2 - top) * FACTOR) * total2
    inverse = 1.0 / (part0 * total0 + part1 + part2)
    part0, part1, part2 = part0 * inverse, part1 * inverse, part2 * inverse
    for i in range(own):
        mine = pl.ds(i * BLOCK, BLOCK)
        row = slice(i, i + 1)
        mixed = (
            sum_ref[mine, :] * part0[row]
            + one_ref[mine, :].astype(jnp.float32) * part1[row]
            + two_ref[mine, :].astype(jnp.float32) * part2[row]
        )
        out_ref[mine, :] = mixed.T.astype(jnp.bfloat16)


def merge(state, one, two):
    rows = state[0].shape[0]
    return pl.pallas_call(
        merge_kernel,
        out_shape=jax.ShapeDtypeStruct((rows, HEAD), jnp.bfloat16),
        in_specs=[VMEM] * 4,
        out_specs=VMEM,
        cost_estimate=cost(8 * rows * HEAD, 10 * rows * HEAD),
        name="merge",
    )(*state, one, two)


def shards(queries, keys, values, allowed):
    rows = queries.shape[0]
    own = rows // BLOCK
    spots = lax.axis_size("blk")
    levels = spots // 2

    def hop(value, target):
        pairs = []
        for i in range(spots):
            high, side = target(i // 2, i % 2)
            if 0 <= high < levels:
                pairs.append((i, high * 2 + side))
        return lax.ppermute(value, "blk", pairs)

    def across(value):
        return hop(value, lambda high, side: (high, 1 - side))

    def swap(value):
        return lax.ppermute(value, "node", [(0, 1), (1, 0)])

    tie = lax.optimization_barrier
    bundled = bundle(keys, values)
    mates = across(queries)
    first = hop(bundled, lambda high, side: (high ^ 1, side))
    second = hop(bundled, lambda high, side: (((high + 1) ^ 1) - 1, side))
    other = swap(bundled)
    table = lists(allowed, own, spots)
    near = (bundled, other)
    state = attend(0, table, queries, near)
    mate_state = attend(1, table, mates, near)
    first, second, mates, mate_state, state = tie((first, second, mates, mate_state, state))
    first_other = swap(first)
    second_other = swap(second)
    guests = hop(mates, lambda high, side: (high + 1 - 2 * side, side))
    beside = (first, first_other, second, second_other)
    mate_part = attend(2, table, mates, beside, mate_state, pack=True)
    one = across(mate_part)
    state = attend(3, table, queries, beside, state)
    guest_part = attend(4, table, guests, beside, pack=True)
    two = hop(guest_part, lambda high, side: (high - 1 + 2 * side, 1 - side))
    return merge(state, one, two)


def solution(mesh):
    placed = (
        P(("grp", "blk", "node"), None),
        P(("grp", "blk", "node"), None),
        P(("grp", "blk", "node"), None),
        P("grp", None),
    )
    return jax.shard_map(
        shards,
        mesh=mesh,
        in_specs=placed,
        out_specs=P(("grp", "blk", "node"), None),
        check_vma=False,
    )
```

```python
import functools
import math

import jax
import jax.numpy as jnp
from jax import lax
from jax.experimental import pallas as pl
from jax.experimental.pallas import tpu as pltpu
from jax.sharding import PartitionSpec as P

HEAD = 128
BLOCK = 128
FLOOR = -1e30
DROP = -3e38
FACTOR = HEAD ** (-0.5) * math.log2(math.e)
COUNT_AT = 64
WIDE = 4

ANY = pl.BlockSpec(memory_space=pl.ANY)
HBM = pl.BlockSpec(memory_space=pltpu.HBM)
VMEM = pl.BlockSpec(memory_space=pltpu.VMEM)
SMEM = pl.BlockSpec(memory_space=pltpu.SMEM)


def cost(flops, moved, exps=0):
    return pl.CostEstimate(flops=flops, bytes_accessed=moved, transcendentals=exps)


def grant(size):
    return pltpu.CompilerParams(vmem_limit_bytes=size << 20)


def bundle_kernel(k_ref, v_ref, out_ref):
    out_ref[0] = k_ref[...]
    for block in range(v_ref.shape[0] // BLOCK):
        at = pl.ds(block * BLOCK, BLOCK)
        out_ref[1, at, :] = v_ref[at, :].T


def bundle(keys, values):
    rows = keys.shape[0]
    return pl.pallas_call(
        bundle_kernel,
        out_shape=jax.ShapeDtypeStruct((2, rows, HEAD), keys.dtype),
        in_specs=[VMEM, VMEM],
        out_specs=VMEM,
        cost_estimate=cost(0, 4 * rows * HEAD * 2),
        compiler_params=grant(4),
        name="bundle",
    )(keys, values)


def list_kernel(spots, own, allowed_ref, out_ref, rows_ref, sems):
    total = rows_ref.shape[1]
    pos = lax.axis_index("blk")
    core = lax.axis_index("node")
    side = pos % 2
    high = pos // 2
    levels = spots // 2
    mate = pos + 1 - 2 * side
    extra = pos - 1 + 2 * side
    extra_ok = (extra >= 0) & (extra < spots)
    first = high + 1 - 2 * (high % 2)
    second = high - 1 + 2 * (high % 2)
    first_ok = (first >= 0) & (first < levels)
    second_ok = (second >= 0) & (second < levels)
    far = high + 1 - 2 * side
    pair = 2 * own
    query_pairs = (pos, mate, jnp.where(extra_ok, extra, 0))
    copies = []
    for group, who in enumerate(query_pairs):
        begin = pl.multiple_of(who * pair + core * own, own)
        copies.append(
            pltpu.make_async_copy(
                allowed_ref.at[pl.ds(begin, own), :],
                rows_ref.at[pl.ds(group * own, own), :],
                sems.at[group],
            )
        )
    for copy in copies:
        copy.start()
    column = lax.broadcasted_iota(jnp.int32, (own, total), 1)
    inside = column % pair
    place = jnp.where(core == 0, inside, (inside + own) % pair)
    owner = column // pair
    none = jnp.int32(-1)
    one = jnp.where(first_ok, first * 2 + side, none)
    two = jnp.where(second_ok, second * 2 + side, none)
    one_x = jnp.where(first_ok & extra_ok & (first == far), one, none)
    two_x = jnp.where(second_ok & extra_ok & (second == far), two, none)
    near = (owner == pos).astype(jnp.int32)
    beside = ((owner == one) | (owner == two)).astype(jnp.int32)
    beyond = ((owner == one_x) | (owner == two_x)).astype(jnp.int32)
    value = place + jnp.where((owner == two) & (near == 0), pair, 0)
    ahead = (
        lax.broadcasted_iota(jnp.int32, (total, total), 0)
        < lax.broadcasted_iota(jnp.int32, (total, total), 1)
    ).astype(jnp.bfloat16)
    for copy in copies:
        copy.wait()
    lane = lax.broadcasted_iota(jnp.int32, (own, 128), 1)
    jobs = ((0, near, 1), (1, near, 1), (1, beside, 2), (0, beside, 2), (2, beyond, 2))
    for job, (group, wanted, widths) in enumerate(jobs):
        kept = (rows_ref[pl.ds(group * own, own), :] > 0).astype(jnp.int32) * wanted
        rank = lax.dot_general(
            kept.astype(jnp.bfloat16),
            ahead,
            (((1,), (0,)), ((), ())),
            preferred_element_type=jnp.float32,
        ).astype(jnp.int32)
        rank = jnp.where(kept > 0, rank, none)
        count = jnp.sum(kept, axis=1, keepdims=True)
        row = jnp.where(lane == COUNT_AT, count, 0)
        for t in range(widths * pair):
            found = jnp.sum(jnp.where(rank == t, value, 0), axis=1, keepdims=True)
            row = jnp.where(lane == t, found, row)
        out_ref[pl.ds(job * own, own), :] = row


def lists(allowed, own, spots):
    return pl.pallas_call(
        functools.partial(list_kernel, spots, own),
        out_shape=jax.ShapeDtypeStruct((5 * own, 128), jnp.int32),
        in_specs=[ANY],
        out_specs=VMEM,
        scratch_shapes=[
            pltpu.VMEM((3 * own, allowed.shape[1]), jnp.int32),
            pltpu.SemaphoreType.DMA((3,)),
        ],
        cost_estimate=cost(1000, 100000),
        compiler_params=grant(4 + allowed.shape[1] ** 2 // 2**16),
        name="lists",
    )(allowed)


def thirds(value):
    high = value.astype(jnp.bfloat16)
    rest = value - high.astype(jnp.float32)
    middle = rest.astype(jnp.bfloat16)
    low = (rest - middle.astype(jnp.float32)).astype(jnp.bfloat16)
    return high, middle, low


def packed_stats(ref, rows):
    own = rows // BLOCK
    pieces = [ref[pl.ds(rows + n * 2 * own, 2 * own), :].astype(jnp.float32) for n in range(3)]
    both = (pieces[2] + pieces[1]) + pieces[0]
    top, total = both[:own], both[own:]
    return jnp.where(total > 0, top, FLOOR), total


def attend_kernel(job, sources, turn, resume, other, pack, list_ref, q_ref, *refs):
    rows = q_ref.shape[0]
    own = rows // BLOCK
    refs = list(refs)
    take = lambda count: [refs.pop(0) for _ in range(count)]
    source_refs = take(sources)
    if not sources:
        k_ref, v_ref = take(2)
    if resume:
        sum_in, stat_in = take(2)
    if other:
        (other_ref,) = take(1)
    (out_ref,) = take(1)
    if not pack:
        (stat_ref,) = take(1)
        sum_ref = out_ref
    (turned_ref,) = take(1) if turn else (q_ref,)
    if sources:
        k_ref, v_ref = take(2)
    if pack:
        sum_ref, stat_ref = take(2)
    (sems,) = refs
    copies = []
    for n, ref in enumerate(source_refs):
        at = pl.ds(n * rows, rows)
        copies.append(pltpu.make_async_copy(ref.at[0], k_ref.at[at, :], sems.at[2 * n]))
        copies.append(pltpu.make_async_copy(ref.at[1], v_ref.at[at, :], sems.at[2 * n + 1]))
    for copy in copies:
        copy.start()
    counts = [list_ref[job * own + i, COUNT_AT] for i in range(own)]
    steps = counts[0]
    for count in counts[1:]:
        steps = jnp.maximum(steps, count)
    steps = (steps + WIDE - 1) // WIDE
    if resume and other:
        top0, total0 = stat_in[pl.ds(0, own), :], stat_in[pl.ds(own, own), :]
        top1, total1 = packed_stats(other_ref, rows)
        top = jnp.maximum(top0, top1)
        part0 = jnp.exp2((top0 - top) * FACTOR)
        part1 = jnp.exp2((top1 - top) * FACTOR) * total1
        stat_ref[pl.ds(0, own), :] = top
        stat_ref[pl.ds(own, own), :] = part0 * total0 + part1
        for i in range(own):
            mine = pl.ds(i * BLOCK, BLOCK)
            row = slice(i, i + 1)
            theirs = other_ref[mine, :].astype(jnp.float32)
            sum_ref[mine, :] = sum_in[mine, :] * part0[row] + theirs * part1[row]
    elif resume:
        sum_ref[...] = sum_in[...]
        stat_ref[...] = stat_in[...]
    else:
        sum_ref[...] = jnp.zeros_like(sum_ref)
        stat_ref[pl.ds(0, own), :] = jnp.full((own, BLOCK), FLOOR, jnp.float32)
        stat_ref[pl.ds(own, own), :] = jnp.zeros((own, BLOCK), jnp.float32)
    if turn:
        for i in range(own):
            mine = pl.ds(i * BLOCK, BLOCK)
            turned_ref[mine, :] = q_ref[mine, :].T
    for copy in copies:
        copy.wait()
    tops = tuple(stat_ref[pl.ds(i, 1), :] for i in range(own))
    totals = tuple(stat_ref[pl.ds(own + i, 1), :] for i in range(own))

    def step(t, state):
        tops, totals = state
        new_tops, new_totals = [], []
        for i in range(own):
            mine = pl.ds(i * BLOCK, BLOCK)
            turned = turned_ref[mine, :]
            spots, scores, biases = [], [], []
            top = tops[i]
            for u in range(WIDE):
                at = t * WIDE + u
                live = at < counts[i]
                index = jnp.where(live, list_ref[job * own + i, at], 0)
                bias = jnp.where(live, jnp.float32(0.0), jnp.float32(DROP))
                spot = pl.ds(pl.multiple_of(index * BLOCK, BLOCK), BLOCK)
                score = jnp.dot(k_ref[spot, :], turned, preferred_element_type=jnp.float32)
                top = jnp.maximum(top, jnp.max(score, axis=0, keepdims=True) + bias)
                spots.append(spot)
                scores.append(score)
                biases.append(bias)
            fade = jnp.exp2((tops[i] - top) * FACTOR)
            total = totals[i] * fade
            part = None
            for spot, score, bias in zip(spots, scores, biases):
                weight = jnp.exp2((score + (bias - top)) * FACTOR)
                total = total + jnp.sum(weight, axis=0, keepdims=True)
                piece = jnp.dot(
                    v_ref[spot, :],
                    weight.astype(jnp.bfloat16),
                    preferred_element_type=jnp.float32,
                )
                part = piece if part is None else part + piece
            sum_ref[mine, :] = sum_ref[mine, :] * fade + part
            new_tops.append(top)
            new_totals.append(total)
        return tuple(new_tops), tuple(new_totals)

    tops, totals = lax.fori_loop(0, steps, step, (tops, totals))
    stats = jnp.concatenate(tops + totals, axis=0)
    if pack:
        for i in range(own):
            mine = pl.ds(i * BLOCK, BLOCK)
            inverse = 1.0 / jnp.maximum(totals[i], 1e-30)
            out_ref[mine, :] = (sum_ref[mine, :] * inverse).astype(jnp.bfloat16)
        for n, piece in enumerate(thirds(stats)):
            out_ref[pl.ds(rows + n * 2 * own, 2 * own), :] = piece
    else:
        stat_ref[...] = stats


def attend(job, table, queries, sources=(), gathered=(), state=(), other=(), turn=False, pack=False):
    rows = queries.shape[0]
    own = rows // BLOCK
    keys = len(sources) * rows if sources else gathered[0].shape[0]
    square = jax.ShapeDtypeStruct((rows, HEAD), queries.dtype)
    sums = jax.ShapeDtypeStruct((rows, HEAD), jnp.float32)
    stats = jax.ShapeDtypeStruct((2 * own, BLOCK), jnp.float32)
    if pack:
        out_shape = [jax.ShapeDtypeStruct((rows + 6 * own, HEAD), jnp.bfloat16)]
        scratch = [pltpu.VMEM(x.shape, x.dtype) for x in (sums, stats)]
    else:
        out_shape = [sums, stats]
        scratch = []
    if turn:
        out_shape.append(square)
    if sources:
        out_shape += [jax.ShapeDtypeStruct((keys, HEAD), queries.dtype)] * 2
    scratch.append(pltpu.SemaphoreType.DMA((max(1, 2 * len(sources)),)))
    direct = [*gathered, *state, *other]
    return pl.pallas_call(
        functools.partial(attend_kernel, job, len(sources), turn, len(state) > 0, len(other) > 0, pack),
        out_shape=out_shape,
        in_specs=[SMEM, VMEM] + [ANY] * len(sources) + [VMEM] * len(direct),
        out_specs=[VMEM] * len(out_shape),
        scratch_shapes=scratch,
        cost_estimate=cost(1 << 20, 1 << 16),
        compiler_params=grant(8),
        name="attend%d" % job,
    )(table, queries, *sources, *direct)


def merge_kernel(sum_ref, stat_ref, other_ref, out_ref):
    rows = sum_ref.shape[0]
    own = rows // BLOCK
    top0, total0 = stat_ref[pl.ds(0, own), :], stat_ref[pl.ds(own, own), :]
    top1, total1 = packed_stats(other_ref, rows)
    top = jnp.maximum(top0, top1)
    part0 = jnp.exp2((top0 - top) * FACTOR)
    part1 = jnp.exp2((top1 - top) * FACTOR) * total1
    inverse = 1.0 / (part0 * total0 + part1)
    part0, part1 = part0 * inverse, part1 * inverse
    for i in range(own):
        mine = pl.ds(i * BLOCK, BLOCK)
        row = slice(i, i + 1)
        theirs = other_ref[mine, :].astype(jnp.float32)
        mixed = sum_ref[mine, :] * part0[row] + theirs * part1[row]
        out_ref[mine, :] = mixed.astype(jnp.bfloat16).T


def merge(state, other):
    rows = state[0].shape[0]
    return pl.pallas_call(
        merge_kernel,
        out_shape=jax.ShapeDtypeStruct((rows, HEAD), jnp.bfloat16),
        in_specs=[VMEM] * 3,
        out_specs=VMEM,
        cost_estimate=cost(8 * rows * HEAD, 10 * rows * HEAD),
        compiler_params=grant(4),
        name="merge",
    )(*state, other)


def shards(queries, keys, values, allowed):
    rows = queries.shape[0]
    own = rows // BLOCK
    spots = lax.axis_size("blk")
    levels = spots // 2

    def hop(value, target):
        pairs = []
        for i in range(spots):
            high, side = target(i // 2, i % 2)
            if 0 <= high < levels:
                pairs.append((i, high * 2 + side))
        return lax.ppermute(value, "blk", pairs)

    def across(value):
        return hop(value, lambda high, side: (high, 1 - side))

    def swap(value):
        return lax.ppermute(value, "node", [(0, 1), (1, 0)])

    tie = lax.optimization_barrier
    bundled = bundle(keys, values)
    mates = across(queries)
    first = hop(bundled, lambda high, side: (high ^ 1, side))
    second = hop(bundled, lambda high, side: (((high + 1) ^ 1) - 1, side))
    other = swap(bundled)
    table = lists(allowed, own, spots)
    *state, turned, near_k, near_v = attend(0, table, queries, (bundled, other), turn=True)
    near = (near_k, near_v)
    *mate_state, mates = attend(1, table, mates, gathered=near, turn=True)
    first, second, mates, mate_state = tie((first, second, mates, mate_state))
    guests = hop(mates, lambda high, side: (high + 1 - 2 * side, side))
    beside = (first, swap(first), second, swap(second))
    mate_part, *beside = attend(2, table, mates, beside, state=mate_state, pack=True)
    one = across(mate_part)
    (guest_part,) = attend(4, table, guests, gathered=beside, pack=True)
    two = hop(guest_part, lambda high, side: (high - 1 + 2 * side, 1 - side))
    state = attend(3, table, turned, gathered=beside, state=state, other=(one,))
    return merge(state, two)


def solution(mesh):
    placed = (
        P(("grp", "blk", "node"), None),
        P(("grp", "blk", "node"), None),
        P(("grp", "blk", "node"), None),
        P("grp", None),
    )
    return jax.shard_map(
        shards,
        mesh=mesh,
        in_specs=placed,
        out_specs=P(("grp", "blk", "node"), None),
        check_vma=False,
    )
```

```python
import functools
import math

import jax
import jax.numpy as jnp
from jax import lax
from jax.experimental import pallas as pl
from jax.experimental.pallas import tpu as pltpu
from jax.sharding import PartitionSpec as P

HEAD = 128
BLOCK = 128
FLOOR = -1e30
DROP = -3e38
FACTOR = HEAD ** (-0.5) * math.log2(math.e)
COUNT_AT = 64
WIDE = 4

ANY = pl.BlockSpec(memory_space=pl.ANY)
HBM = pl.BlockSpec(memory_space=pltpu.HBM)
VMEM = pl.BlockSpec(memory_space=pltpu.VMEM)
SMEM = pl.BlockSpec(memory_space=pltpu.SMEM)


def cost(flops, moved, exps=0):
    return pl.CostEstimate(flops=flops, bytes_accessed=moved, transcendentals=exps)


def grant(size):
    return pltpu.CompilerParams(vmem_limit_bytes=size << 20)


def bundle_kernel(q_ref, k_ref, v_ref, out_ref, turned_ref, raw_q_ref, raw_v_ref, sems):
    load_v = pltpu.make_async_copy(v_ref, raw_v_ref, sems.at[0])
    load_k = pltpu.make_async_copy(k_ref, out_ref.at[0], sems.at[1])
    load_q = pltpu.make_async_copy(q_ref, raw_q_ref, sems.at[2])
    load_v.start()
    load_k.start()
    load_q.start()
    blocks = [pl.ds(n * BLOCK, BLOCK) for n in range(raw_v_ref.shape[0] // BLOCK)]
    load_v.wait()
    for at in blocks:
        out_ref[1, at, :] = raw_v_ref[at, :].T
    load_q.wait()
    for at in blocks:
        turned_ref[at, :] = raw_q_ref[at, :].T
    load_k.wait()


def bundle(queries, keys, values):
    rows = keys.shape[0]
    operands = [
        pltpu.with_memory_space_constraint(x, pltpu.MemorySpace.HBM)
        for x in (queries, keys, values)
    ]
    return pl.pallas_call(
        bundle_kernel,
        out_shape=(
            jax.ShapeDtypeStruct((2, rows, HEAD), keys.dtype),
            jax.ShapeDtypeStruct((rows, HEAD), queries.dtype),
        ),
        in_specs=[HBM] * 3,
        out_specs=[VMEM] * 2,
        scratch_shapes=[
            pltpu.VMEM((rows, HEAD), queries.dtype),
            pltpu.VMEM((rows, HEAD), values.dtype),
            pltpu.SemaphoreType.DMA((3,)),
        ],
        cost_estimate=cost(0, 4 * rows * HEAD * 2),
        compiler_params=grant(4),
        name="bundle",
    )(*operands)


def list_kernel(spots, own, allowed_ref, out_ref, rows_ref, sems):
    total = rows_ref.shape[1]
    pos = lax.axis_index("blk")
    core = lax.axis_index("node")
    side = pos % 2
    high = pos // 2
    levels = spots // 2
    mate = pos + 1 - 2 * side
    extra = pos - 1 + 2 * side
    extra_ok = (extra >= 0) & (extra < spots)
    first = high + 1 - 2 * (high % 2)
    second = high - 1 + 2 * (high % 2)
    first_ok = (first >= 0) & (first < levels)
    second_ok = (second >= 0) & (second < levels)
    far = high + 1 - 2 * side
    pair = 2 * own
    query_pairs = (pos, mate, jnp.where(extra_ok, extra, 0))
    copies = []
    for group, who in enumerate(query_pairs):
        begin = pl.multiple_of(who * pair + core * own, own)
        copies.append(
            pltpu.make_async_copy(
                allowed_ref.at[pl.ds(begin, own), :],
                rows_ref.at[pl.ds(group * own, own), :],
                sems.at[group],
            )
        )
    for copy in copies:
        copy.start()
    column = lax.broadcasted_iota(jnp.int32, (own, total), 1)
    inside = column % pair
    place = jnp.where(core == 0, inside, (inside + own) % pair)
    owner = column // pair
    none = jnp.int32(-1)
    one = jnp.where(first_ok, first * 2 + side, none)
    two = jnp.where(second_ok, second * 2 + side, none)
    one_x = jnp.where(first_ok & extra_ok & (first == far), one, none)
    two_x = jnp.where(second_ok & extra_ok & (second == far), two, none)
    near = (owner == pos).astype(jnp.int32)
    beside = ((owner == one) | (owner == two)).astype(jnp.int32)
    beyond = ((owner == one_x) | (owner == two_x)).astype(jnp.int32)
    later = (inside >= own) != (owner == two)
    value = place + jnp.where(later & (near == 0), pair, 0)
    ahead = (
        lax.broadcasted_iota(jnp.int32, (total, total), 0)
        < lax.broadcasted_iota(jnp.int32, (total, total), 1)
    ).astype(jnp.bfloat16)
    for copy in copies:
        copy.wait()
    lane = lax.broadcasted_iota(jnp.int32, (own, 128), 1)
    jobs = ((0, near, 1), (1, near, 1), (1, beside, 2), (0, beside, 2), (2, beyond, 2))
    for job, (group, wanted, widths) in enumerate(jobs):
        kept = (rows_ref[pl.ds(group * own, own), :] > 0).astype(jnp.int32) * wanted
        rank = lax.dot_general(
            kept.astype(jnp.bfloat16),
            ahead,
            (((1,), (0,)), ((), ())),
            preferred_element_type=jnp.float32,
        ).astype(jnp.int32)
        rank = jnp.where(kept > 0, rank, none)
        count = jnp.sum(kept, axis=1, keepdims=True)
        row = jnp.where(lane == COUNT_AT, count, 0)
        for t in range(widths * pair):
            found = jnp.sum(jnp.where(rank == t, value, 0), axis=1, keepdims=True)
            row = jnp.where(lane == t, found, row)
        out_ref[pl.ds(job * own, own), :] = row


def lists(allowed, own, spots):
    return pl.pallas_call(
        functools.partial(list_kernel, spots, own),
        out_shape=jax.ShapeDtypeStruct((5 * own, 128), jnp.int32),
        in_specs=[ANY],
        out_specs=VMEM,
        scratch_shapes=[
            pltpu.VMEM((3 * own, allowed.shape[1]), jnp.int32),
            pltpu.SemaphoreType.DMA((3,)),
        ],
        cost_estimate=cost(1000, 100000),
        compiler_params=grant(4 + allowed.shape[1] ** 2 // 2**16),
        name="lists",
    )(allowed)


def thirds(value):
    high = value.astype(jnp.bfloat16)
    rest = value - high.astype(jnp.float32)
    middle = rest.astype(jnp.bfloat16)
    low = (rest - middle.astype(jnp.float32)).astype(jnp.bfloat16)
    return high, middle, low


def packed_stats(ref, rows):
    own = rows // BLOCK
    pieces = [ref[pl.ds(rows + n * 2 * own, 2 * own), :].astype(jnp.float32) for n in range(3)]
    both = (pieces[2] + pieces[1]) + pieces[0]
    top, total = both[:own], both[own:]
    return jnp.where(total > 0, top, FLOOR), total


def attend_kernel(job, sources, turn, resume, other, pack, list_ref, q_ref, *refs):
    rows = q_ref.shape[0]
    own = rows // BLOCK
    refs = list(refs)
    take = lambda count: [refs.pop(0) for _ in range(count)]
    source_refs = take(sources)
    if not sources:
        k_ref, v_ref = take(2)
    if resume:
        sum_in, stat_in = take(2)
    if other:
        (other_ref,) = take(1)
    (out_ref,) = take(1)
    if not pack:
        (stat_ref,) = take(1)
        sum_ref = out_ref
    (turned_ref,) = take(1) if turn else (q_ref,)
    if sources:
        k_ref, v_ref = take(2)
    if pack:
        sum_ref, stat_ref = take(2)
    (sems,) = refs
    copies = []
    for n, ref in enumerate(source_refs):
        at = pl.ds(n * rows, rows)
        copies.append(pltpu.make_async_copy(ref.at[0], k_ref.at[at, :], sems.at[2 * n]))
        copies.append(pltpu.make_async_copy(ref.at[1], v_ref.at[at, :], sems.at[2 * n + 1]))
    for copy in copies:
        copy.start()
    counts = [list_ref[job * own + i, COUNT_AT] for i in range(own)]
    steps = counts[0]
    for count in counts[1:]:
        steps = jnp.maximum(steps, count)
    steps = (steps + WIDE - 1) // WIDE
    if resume and other:
        top0, total0 = stat_in[pl.ds(0, own), :], stat_in[pl.ds(own, own), :]
        top1, total1 = packed_stats(other_ref, rows)
        top = jnp.maximum(top0, top1)
        part0 = jnp.exp2((top0 - top) * FACTOR)
        part1 = jnp.exp2((top1 - top) * FACTOR) * total1
        stat_ref[pl.ds(0, own), :] = top
        stat_ref[pl.ds(own, own), :] = part0 * total0 + part1
        for i in range(own):
            mine = pl.ds(i * BLOCK, BLOCK)
            row = slice(i, i + 1)
            theirs = other_ref[mine, :].astype(jnp.float32)
            sum_ref[mine, :] = sum_in[mine, :] * part0[row] + theirs * part1[row]
    elif resume:
        sum_ref[...] = sum_in[...]
        stat_ref[...] = stat_in[...]
    else:
        sum_ref[...] = jnp.zeros_like(sum_ref)
        stat_ref[pl.ds(0, own), :] = jnp.full((own, BLOCK), FLOOR, jnp.float32)
        stat_ref[pl.ds(own, own), :] = jnp.zeros((own, BLOCK), jnp.float32)
    if turn:
        for i in range(own):
            mine = pl.ds(i * BLOCK, BLOCK)
            turned_ref[mine, :] = q_ref[mine, :].T
    for copy in copies:
        copy.wait()
    tops = tuple(stat_ref[pl.ds(i, 1), :] for i in range(own))
    totals = tuple(stat_ref[pl.ds(own + i, 1), :] for i in range(own))

    def step(t, state):
        tops, totals = state
        new_tops, new_totals = [], []
        for i in range(own):
            mine = pl.ds(i * BLOCK, BLOCK)
            turned = turned_ref[mine, :]
            spots, scores, biases = [], [], []
            top = tops[i]
            for u in range(WIDE):
                at = t * WIDE + u
                live = at < counts[i]
                index = jnp.where(live, list_ref[job * own + i, at], 0)
                bias = jnp.where(live, jnp.float32(0.0), jnp.float32(DROP))
                spot = pl.ds(pl.multiple_of(index * BLOCK, BLOCK), BLOCK)
                score = jnp.dot(k_ref[spot, :], turned, preferred_element_type=jnp.float32)
                top = jnp.maximum(top, jnp.max(score, axis=0, keepdims=True) + bias)
                spots.append(spot)
                scores.append(score)
                biases.append(bias)
            fade = jnp.exp2((tops[i] - top) * FACTOR)
            total = totals[i] * fade
            part = None
            for spot, score, bias in zip(spots, scores, biases):
                weight = jnp.exp2((score + (bias - top)) * FACTOR)
                total = total + jnp.sum(weight, axis=0, keepdims=True)
                piece = jnp.dot(
                    v_ref[spot, :],
                    weight.astype(jnp.bfloat16),
                    preferred_element_type=jnp.float32,
                )
                part = piece if part is None else part + piece
            sum_ref[mine, :] = sum_ref[mine, :] * fade + part
            new_tops.append(top)
            new_totals.append(total)
        return tuple(new_tops), tuple(new_totals)

    tops, totals = lax.fori_loop(0, steps, step, (tops, totals))
    stats = jnp.concatenate(tops + totals, axis=0)
    if pack:
        for i in range(own):
            mine = pl.ds(i * BLOCK, BLOCK)
            inverse = 1.0 / jnp.maximum(totals[i], 1e-30)
            out_ref[mine, :] = (sum_ref[mine, :] * inverse).astype(jnp.bfloat16)
        for n, piece in enumerate(thirds(stats)):
            out_ref[pl.ds(rows + n * 2 * own, 2 * own), :] = piece
    else:
        stat_ref[...] = stats


def attend(job, table, queries, sources=(), gathered=(), state=(), other=(), turn=False, pack=False, spare=0):
    rows = queries.shape[0]
    own = rows // BLOCK
    keys = len(sources) * rows if sources else gathered[0].shape[0]
    square = jax.ShapeDtypeStruct((rows, HEAD), queries.dtype)
    sums = jax.ShapeDtypeStruct((rows, HEAD), jnp.float32)
    stats = jax.ShapeDtypeStruct((2 * own, BLOCK), jnp.float32)
    if pack:
        out_shape = [jax.ShapeDtypeStruct((rows + 6 * own + 16 * spare, HEAD), jnp.bfloat16)]
        scratch = [pltpu.VMEM(x.shape, x.dtype) for x in (sums, stats)]
    else:
        out_shape = [sums, stats]
        scratch = []
    if turn:
        out_shape.append(square)
    if sources:
        out_shape += [jax.ShapeDtypeStruct((keys, HEAD), queries.dtype)] * 2
    scratch.append(pltpu.SemaphoreType.DMA((max(1, 2 * len(sources)),)))
    direct = [*gathered, *state, *other]
    return pl.pallas_call(
        functools.partial(attend_kernel, job, len(sources), turn, len(state) > 0, len(other) > 0, pack),
        out_shape=out_shape,
        in_specs=[SMEM, VMEM] + [ANY] * len(sources) + [VMEM] * len(direct),
        out_specs=[VMEM] * len(out_shape),
        scratch_shapes=scratch,
        cost_estimate=cost(1 << 20, 1 << 16),
        compiler_params=grant(8),
        name="attend%d" % job,
    )(table, queries, *sources, *direct)


def merge_kernel(sum_ref, stat_ref, *refs):
    *other_refs, out_ref = refs
    rows = sum_ref.shape[0]
    own = rows // BLOCK
    top0, total0 = stat_ref[pl.ds(0, own), :], stat_ref[pl.ds(own, own), :]
    others = [packed_stats(ref, rows) for ref in other_refs]
    top = top0
    for their_top, _ in others:
        top = jnp.maximum(top, their_top)
    share = jnp.exp2((top0 - top) * FACTOR)
    shares = [jnp.exp2((a - top) * FACTOR) * b for a, b in others]
    inverse = 1.0 / sum(shares, share * total0)
    share = share * inverse
    shares = [x * inverse for x in shares]
    for i in range(own):
        mine = pl.ds(i * BLOCK, BLOCK)
        row = slice(i, i + 1)
        mixed = sum_ref[mine, :] * share[row]
        for ref, part in zip(other_refs, shares):
            mixed = mixed + ref[mine, :].astype(jnp.float32) * part[row]
        out_ref[mine, :] = mixed.astype(jnp.bfloat16).T


def merge(state, *others):
    rows = state[0].shape[0]
    return pl.pallas_call(
        merge_kernel,
        out_shape=jax.ShapeDtypeStruct((rows, HEAD), jnp.bfloat16),
        in_specs=[VMEM] * (2 + len(others)),
        out_specs=VMEM,
        cost_estimate=cost(8 * rows * HEAD, 10 * rows * HEAD),
        compiler_params=grant(4),
        name="merge",
    )(*state, *others)


def shards(queries, keys, values, allowed):
    rows = queries.shape[0]
    own = rows // BLOCK
    spots = lax.axis_size("blk")
    levels = spots // 2

    def hop(value, target):
        pairs = []
        for i in range(spots):
            high, side = target(i // 2, i % 2)
            if 0 <= high < levels:
                pairs.append((i, high * 2 + side))
        return lax.ppermute(value, "blk", pairs)

    def across(value):
        return hop(value, lambda high, side: (high, 1 - side))

    def swap(value):
        return lax.ppermute(value, "node", [(0, 1), (1, 0)])

    def trade(value, turn):
        pairs = []
        for i in range(spots):
            high, side = i // 2, i % 2
            for core in range(2):
                far = (high ^ 1) if core == turn else ((high + 1) ^ 1) - 1
                if 0 <= far < levels:
                    pairs.append((2 * i + core, 2 * (far * 2 + side) + core))
        return lax.ppermute(value, ("blk", "node"), pairs)

    def visit(value):
        pairs = []
        for i in range(spots):
            high, side = i // 2, i % 2
            for core in range(2):
                came = side if core == 0 else 1 - side
                far = high + 1 - 2 * came
                if 0 < far < levels - 1:
                    pairs.append((2 * i + core, 2 * (far * 2 + came) + core))
        return lax.ppermute(value, ("blk", "node"), pairs)

    tie = lax.optimization_barrier
    bundled, turned = bundle(queries, keys, values)
    mates = across(turned)
    first = trade(bundled, 0)
    second = trade(bundled, 1)
    other = swap(bundled)
    table = lists(allowed, own, spots)
    *state, near_k, near_v = attend(0, table, turned, (bundled, other))
    near = (near_k, near_v)
    mate_state = attend(1, table, mates, gathered=near)
    core = lax.axis_index("node")
    parcel = jnp.where(core == 0, mates, turned)
    first, second, mates, mate_state = tie((first, second, mates, mate_state))
    guests = visit(parcel)
    beside = (first, swap(first), second, swap(second))
    mate_part, *beside = attend(2, table, mates, beside, state=mate_state, pack=True, spare=2)
    one = across(mate_part)
    (guest_part,) = attend(4, table, guests, gathered=beside, pack=True)
    homeward = []
    for i in range(2, spots - 2):
        high, side = i // 2, i % 2
        homeward.append((i, (high - 1 + 2 * side) * 2 + 1 - side))
    two = lax.ppermute(guest_part, "blk", homeward)
    state = attend(3, table, turned, gathered=beside, state=state)
    return merge(state, one, two)


def solution(mesh):
    placed = (
        P(("grp", "blk", "node"), None),
        P(("grp", "blk", "node"), None),
        P(("grp", "blk", "node"), None),
        P("grp", None),
    )
    return jax.shard_map(
        shards,
        mesh=mesh,
        in_specs=placed,
        out_specs=P(("grp", "blk", "node"), None),
        check_vma=False,
    )
```

```python
import functools
import math

import jax
import jax.numpy as jnp
from jax import lax
from jax.experimental import pallas as pl
from jax.experimental.pallas import tpu as pltpu
from jax.sharding import PartitionSpec as P

HEAD = 128
BLOCK = 128
FLOOR = -1e30
DROP = -3e38
FACTOR = HEAD ** (-0.5) * math.log2(math.e)
COUNT_AT = 64
WIDE = 4

ANY = pl.BlockSpec(memory_space=pl.ANY)
HBM = pl.BlockSpec(memory_space=pltpu.HBM)
VMEM = pl.BlockSpec(memory_space=pltpu.VMEM)
SMEM = pl.BlockSpec(memory_space=pltpu.SMEM)


def cost(flops, moved, exps=0):
    return pl.CostEstimate(flops=flops, bytes_accessed=moved, transcendentals=exps)


def grant(size):
    return pltpu.CompilerParams(vmem_limit_bytes=size << 20)


def bundle_kernel(q_ref, k_ref, v_ref, out_ref, turned_ref, raw_q_ref, raw_v_ref, sems):
    load_v = pltpu.make_async_copy(v_ref, raw_v_ref, sems.at[0])
    load_k = pltpu.make_async_copy(k_ref, out_ref.at[0], sems.at[1])
    load_q = pltpu.make_async_copy(q_ref, raw_q_ref, sems.at[2])
    load_v.start()
    load_k.start()
    load_q.start()
    blocks = [pl.ds(n * BLOCK, BLOCK) for n in range(raw_v_ref.shape[0] // BLOCK)]
    load_v.wait()
    for at in blocks:
        out_ref[1, at, :] = raw_v_ref[at, :].T
    load_q.wait()
    for at in blocks:
        turned_ref[at, :] = raw_q_ref[at, :].T
    load_k.wait()


def bundle(queries, keys, values):
    rows = keys.shape[0]
    operands = [
        pltpu.with_memory_space_constraint(x, pltpu.MemorySpace.HBM)
        for x in (queries, keys, values)
    ]
    return pl.pallas_call(
        bundle_kernel,
        out_shape=(
            jax.ShapeDtypeStruct((2, rows, HEAD), keys.dtype),
            jax.ShapeDtypeStruct((rows, HEAD), queries.dtype),
        ),
        in_specs=[HBM] * 3,
        out_specs=[VMEM] * 2,
        scratch_shapes=[
            pltpu.VMEM((rows, HEAD), queries.dtype),
            pltpu.VMEM((rows, HEAD), values.dtype),
            pltpu.SemaphoreType.DMA((3,)),
        ],
        cost_estimate=cost(0, 4 * rows * HEAD * 2),
        compiler_params=grant(4),
        name="bundle",
    )(*operands)


def list_kernel(spots, own, allowed_ref, out_ref, rows_ref, sems):
    total = rows_ref.shape[1]
    pos = lax.axis_index("blk")
    core = lax.axis_index("node")
    side = pos % 2
    high = pos // 2
    levels = spots // 2
    mate = pos + 1 - 2 * side
    extra = pos - 1 + 2 * side
    extra_ok = (extra >= 0) & (extra < spots)
    first = high + 1 - 2 * (high % 2)
    second = high - 1 + 2 * (high % 2)
    first_ok = (first >= 0) & (first < levels)
    second_ok = (second >= 0) & (second < levels)
    far = high + 1 - 2 * side
    pair = 2 * own
    query_pairs = (pos, mate, jnp.where(extra_ok, extra, 0))
    copies = []
    for group, who in enumerate(query_pairs):
        begin = pl.multiple_of(who * pair + core * own, own)
        copies.append(
            pltpu.make_async_copy(
                allowed_ref.at[pl.ds(begin, own), :],
                rows_ref.at[pl.ds(group * own, own), :],
                sems.at[group],
            )
        )
    for copy in copies:
        copy.start()
    column = lax.broadcasted_iota(jnp.int32, (own, total), 1)
    inside = column % pair
    place = jnp.where(core == 0, inside, (inside + own) % pair)
    owner = column // pair
    none = jnp.int32(-1)
    one = jnp.where(first_ok, first * 2 + side, none)
    two = jnp.where(second_ok, second * 2 + side, none)
    one_x = jnp.where(first_ok & extra_ok & (first == far), one, none)
    two_x = jnp.where(second_ok & extra_ok & (second == far), two, none)
    near = (owner == pos).astype(jnp.int32)
    beside = ((owner == one) | (owner == two)).astype(jnp.int32)
    beyond = ((owner == one_x) | (owner == two_x)).astype(jnp.int32)
    later = (inside >= own) != (owner == two)
    value = place + jnp.where(later & (near == 0), pair, 0)
    ahead = (
        lax.broadcasted_iota(jnp.int32, (total, total), 0)
        < lax.broadcasted_iota(jnp.int32, (total, total), 1)
    ).astype(jnp.bfloat16)
    for copy in copies:
        copy.wait()
    lane = lax.broadcasted_iota(jnp.int32, (own, 128), 1)
    jobs = ((0, near, 1), (1, near, 1), (1, beside, 2), (0, beside, 2), (2, beyond, 2))
    for job, (group, wanted, widths) in enumerate(jobs):
        kept = (rows_ref[pl.ds(group * own, own), :] > 0).astype(jnp.int32) * wanted
        rank = lax.dot_general(
            kept.astype(jnp.bfloat16),
            ahead,
            (((1,), (0,)), ((), ())),
            preferred_element_type=jnp.float32,
        ).astype(jnp.int32)
        rank = jnp.where(kept > 0, rank, none)
        count = jnp.sum(kept, axis=1, keepdims=True)
        row = jnp.where(lane == COUNT_AT, count, 0)
        for t in range(widths * pair):
            found = jnp.sum(jnp.where(rank == t, value, 0), axis=1, keepdims=True)
            row = jnp.where(lane == t, found, row)
        out_ref[pl.ds(job * own, own), :] = row


def lists(allowed, own, spots):
    return pl.pallas_call(
        functools.partial(list_kernel, spots, own),
        out_shape=jax.ShapeDtypeStruct((5 * own, 128), jnp.int32),
        in_specs=[ANY],
        out_specs=VMEM,
        scratch_shapes=[
            pltpu.VMEM((3 * own, allowed.shape[1]), jnp.int32),
            pltpu.SemaphoreType.DMA((3,)),
        ],
        cost_estimate=cost(1000, 100000),
        compiler_params=grant(4 + allowed.shape[1] ** 2 // 2**16),
        name="lists",
    )(allowed)


def thirds(value):
    high = value.astype(jnp.bfloat16)
    rest = value - high.astype(jnp.float32)
    middle = rest.astype(jnp.bfloat16)
    low = (rest - middle.astype(jnp.float32)).astype(jnp.bfloat16)
    return high, middle, low


def packed_stats(ref, rows):
    own = rows // BLOCK
    pieces = [ref[pl.ds(rows + n * 2 * own, 2 * own), :].astype(jnp.float32) for n in range(3)]
    both = (pieces[2] + pieces[1]) + pieces[0]
    top, total = both[:own], both[own:]
    return jnp.where(total > 0, top, FLOOR), total


def attend_kernel(base, sources, resume, pack, list_ref, q_ref, *refs):
    rows = q_ref.shape[0]
    own = rows // BLOCK
    refs = list(refs)
    take = lambda count: [refs.pop(0) for _ in range(count)]
    source_refs = take(sources)
    if not sources:
        k_ref, v_ref = take(2)
    if resume:
        take(2)
    if pack:
        (out_ref,) = take(1)
    if sources:
        k_ref, v_ref = take(2)
    sum_ref, stat_ref, sems = refs
    copies = []
    for n, ref in enumerate(source_refs):
        at = pl.ds(n * rows, rows)
        copies.append(pltpu.make_async_copy(ref.at[0], k_ref.at[at, :], sems.at[2 * n]))
        copies.append(pltpu.make_async_copy(ref.at[1], v_ref.at[at, :], sems.at[2 * n + 1]))
    for copy in copies:
        copy.start()
    counts = [list_ref[base + i, COUNT_AT] for i in range(own)]
    steps = counts[0]
    for count in counts[1:]:
        steps = jnp.maximum(steps, count)
    steps = (steps + WIDE - 1) // WIDE
    if not resume:
        sum_ref[...] = jnp.zeros_like(sum_ref)
        stat_ref[pl.ds(0, own), :] = jnp.full((own, BLOCK), FLOOR, jnp.float32)
        stat_ref[pl.ds(own, own), :] = jnp.zeros((own, BLOCK), jnp.float32)
    for copy in copies:
        copy.wait()
    tops = tuple(stat_ref[pl.ds(i, 1), :] for i in range(own))
    totals = tuple(stat_ref[pl.ds(own + i, 1), :] for i in range(own))

    def step(t, state):
        tops, totals = state
        new_tops, new_totals = [], []
        for i in range(own):
            mine = pl.ds(i * BLOCK, BLOCK)
            turned = q_ref[mine, :]
            spots, scores, biases = [], [], []
            top = tops[i]
            for u in range(WIDE):
                at = t * WIDE + u
                live = at < counts[i]
                index = jnp.where(live, list_ref[base + i, at], 0)
                bias = jnp.where(live, jnp.float32(0.0), jnp.float32(DROP))
                spot = pl.ds(pl.multiple_of(index * BLOCK, BLOCK), BLOCK)
                score = jnp.dot(k_ref[spot, :], turned, preferred_element_type=jnp.float32)
                top = jnp.maximum(top, jnp.max(score, axis=0, keepdims=True) + bias)
                spots.append(spot)
                scores.append(score)
                biases.append(bias)
            fade = jnp.exp2((tops[i] - top) * FACTOR)
            total, part = totals[i] * fade, None
            for spot, score, bias in zip(spots, scores, biases):
                weight = jnp.exp2((score + (bias - top)) * FACTOR)
                total = total + jnp.sum(weight, axis=0, keepdims=True)
                piece = jnp.dot(
                    v_ref[spot, :],
                    weight.astype(jnp.bfloat16),
                    preferred_element_type=jnp.float32,
                )
                part = piece if part is None else part + piece
            sum_ref[mine, :] = sum_ref[mine, :] * fade + part
            new_tops.append(top)
            new_totals.append(total)
        return tuple(new_tops), tuple(new_totals)

    tops, totals = lax.fori_loop(0, steps, step, (tops, totals))
    stats = jnp.concatenate(tops + totals, axis=0)
    if not pack:
        stat_ref[...] = stats
    else:
        for i in range(own):
            mine = pl.ds(i * BLOCK, BLOCK)
            inverse = 1.0 / jnp.maximum(totals[i], 1e-30)
            out_ref[mine, :] = (sum_ref[mine, :] * inverse).astype(jnp.bfloat16)
        for n, piece in enumerate(thirds(stats)):
            out_ref[pl.ds(rows + n * 2 * own, 2 * own), :] = piece
        spare = out_ref.shape[0] - rows - 6 * own
        if spare:
            out_ref[pl.ds(rows + 6 * own, spare), :] = jnp.zeros((spare, HEAD), out_ref.dtype)


def attend(job, table, queries, sources=(), gathered=(), state=(), pack=False, spare=0):
    rows = queries.shape[0]
    own = rows // BLOCK
    keys = len(sources) * rows if sources else gathered[0].shape[0]
    out_shape = []
    if pack:
        height = rows + 6 * own + 16 * spare
        out_shape.append(jax.ShapeDtypeStruct((height, HEAD), jnp.bfloat16))
    if sources:
        out_shape += [jax.ShapeDtypeStruct((keys, HEAD), queries.dtype)] * 2
    kept = [
        jax.ShapeDtypeStruct((rows, HEAD), jnp.float32),
        jax.ShapeDtypeStruct((2 * own, BLOCK), jnp.float32),
    ]
    scratch = []
    if pack and not state:
        scratch = [pltpu.VMEM(x.shape, x.dtype) for x in kept]
    else:
        out_shape += kept
    direct = [*gathered, *state]
    operands = 2 + len(sources) + len(direct)
    outs = len(out_shape)
    aliases = {operands - 2: outs - 2, operands - 1: outs - 1} if state else {}
    return pl.pallas_call(
        functools.partial(attend_kernel, job * own, len(sources), len(state) > 0, pack),
        out_shape=out_shape,
        in_specs=[SMEM, VMEM] + [ANY] * len(sources) + [VMEM] * len(direct),
        out_specs=[VMEM] * outs,
        scratch_shapes=scratch + [pltpu.SemaphoreType.DMA((max(1, 2 * len(sources)),))],
        input_output_aliases=aliases,
        cost_estimate=cost(1 << 20, 1 << 16),
        compiler_params=grant(8),
        name="attend%d" % job,
    )(table, queries, *sources, *direct)


def choose_kernel(one_ref, two_ref, out_ref):
    core = lax.axis_index("node")

    @pl.when(core == 0)
    def _():
        out_ref[...] = one_ref[...]

    @pl.when(core != 0)
    def _():
        out_ref[...] = two_ref[...]


def choose(one, two):
    return pl.pallas_call(
        choose_kernel,
        out_shape=jax.ShapeDtypeStruct(one.shape, one.dtype),
        in_specs=[VMEM] * 2,
        out_specs=VMEM,
        cost_estimate=cost(1 << 10, 1 << 10),
        compiler_params=grant(1),
        name="choose",
    )(one, two)


def merge_kernel(sum_ref, stat_ref, *refs):
    *other_refs, out_ref = refs
    rows = sum_ref.shape[0]
    own = rows // BLOCK
    top0, total0 = stat_ref[pl.ds(0, own), :], stat_ref[pl.ds(own, own), :]
    others = [packed_stats(ref, rows) for ref in other_refs]
    top = top0
    for their_top, _ in others:
        top = jnp.maximum(top, their_top)
    share = jnp.exp2((top0 - top) * FACTOR)
    shares = [jnp.exp2((a - top) * FACTOR) * b for a, b in others]
    inverse = 1.0 / sum(shares, share * total0)
    share = share * inverse
    shares = [x * inverse for x in shares]
    for i in range(own):
        mine = pl.ds(i * BLOCK, BLOCK)
        row = slice(i, i + 1)
        mixed = sum_ref[mine, :] * share[row]
        for ref, part in zip(other_refs, shares):
            mixed = mixed + ref[mine, :].astype(jnp.float32) * part[row]
        out_ref[mine, :] = mixed.astype(jnp.bfloat16).T


def merge(state, *others):
    rows = state[0].shape[0]
    return pl.pallas_call(
        merge_kernel,
        out_shape=jax.ShapeDtypeStruct((rows, HEAD), jnp.bfloat16),
        in_specs=[VMEM] * (2 + len(others)),
        out_specs=VMEM,
        cost_estimate=cost(8 * rows * HEAD, 10 * rows * HEAD),
        compiler_params=grant(4),
        name="merge",
    )(*state, *others)


def shards(queries, keys, values, allowed):
    rows = queries.shape[0]
    own = rows // BLOCK
    spots = lax.axis_size("blk")
    levels = spots // 2

    def hop(value, target):
        pairs = []
        for i in range(spots):
            high, side = target(i // 2, i % 2)
            if 0 <= high < levels:
                pairs.append((i, high * 2 + side))
        return lax.ppermute(value, "blk", pairs)

    def across(value):
        return hop(value, lambda high, side: (high, 1 - side))

    def swap(value):
        return lax.ppermute(value, "node", [(0, 1), (1, 0)])

    def trade(value, turn):
        pairs = []
        for i in range(spots):
            high, side = i // 2, i % 2
            for core in range(2):
                far = (high ^ 1) if core == turn else ((high + 1) ^ 1) - 1
                if 0 <= far < levels:
                    pairs.append((2 * i + core, 2 * (far * 2 + side) + core))
        return lax.ppermute(value, ("blk", "node"), pairs)

    def visit(value):
        pairs = []
        for i in range(spots):
            high, side = i // 2, i % 2
            for core in range(2):
                came = side if core == 0 else 1 - side
                far = high + 1 - 2 * came
                if 0 < far < levels - 1:
                    pairs.append((2 * i + core, 2 * (far * 2 + came) + core))
        return lax.ppermute(value, ("blk", "node"), pairs)

    tie = lax.optimization_barrier
    bundled, turned = bundle(queries, keys, values)
    mates = across(turned)
    first = trade(bundled, 0)
    second = trade(bundled, 1)
    other = swap(bundled)
    table = lists(allowed, own, spots)
    *near, sums, stats = attend(0, table, turned, (bundled, other))
    mate_state = attend(1, table, mates, gathered=near)
    parcel = choose(mates, turned)
    first, second, mates, mate_state = tie((first, second, mates, mate_state))
    guests = visit(parcel)
    beside = (first, swap(first), second, swap(second))
    mate_part, *beside, _, _ = attend(2, table, mates, beside, state=mate_state, pack=True, spare=2)
    one = across(mate_part)
    state = attend(3, table, turned, gathered=beside, state=(sums, stats))
    (guest_part,) = attend(4, table, guests, gathered=beside, pack=True)
    homeward = []
    for i in range(2, spots - 2):
        high, side = i // 2, i % 2
        homeward.append((i, (high - 1 + 2 * side) * 2 + 1 - side))
    two = lax.ppermute(guest_part, "blk", homeward)
    return merge(state, one, two)


def solution(mesh):
    placed = (
        P(("grp", "blk", "node"), None),
        P(("grp", "blk", "node"), None),
        P(("grp", "blk", "node"), None),
        P("grp", None),
    )
    return jax.shard_map(
        shards,
        mesh=mesh,
        in_specs=placed,
        out_specs=P(("grp", "blk", "node"), None),
        check_vma=False,
    )
```

```python
import functools
import math

import jax
import jax.numpy as jnp
from jax import lax
from jax.experimental import pallas as pl
from jax.experimental.pallas import tpu as pltpu
from jax.sharding import PartitionSpec as P

HEAD = 128
BLOCK = 128
FLOOR = -1e30
DROP = -3e38
FACTOR = HEAD ** (-0.5) * math.log2(math.e)
COUNT_AT = 64
WIDE = 4

ANY = pl.BlockSpec(memory_space=pl.ANY)
HBM = pl.BlockSpec(memory_space=pltpu.HBM)
VMEM = pl.BlockSpec(memory_space=pltpu.VMEM)


def cost(flops, moved, exps=0):
    return pl.CostEstimate(flops=flops, bytes_accessed=moved, transcendentals=exps)


def grant(size):
    return pltpu.CompilerParams(vmem_limit_bytes=size << 20)


def bundle_kernel(q_ref, k_ref, v_ref, out_ref, turned_ref, raw_q_ref, raw_v_ref, sems):
    load_v = pltpu.make_async_copy(v_ref, raw_v_ref, sems.at[0])
    load_k = pltpu.make_async_copy(k_ref, out_ref.at[0], sems.at[1])
    load_q = pltpu.make_async_copy(q_ref, raw_q_ref, sems.at[2])
    load_v.start()
    load_k.start()
    load_q.start()
    blocks = [pl.ds(n * BLOCK, BLOCK) for n in range(raw_v_ref.shape[0] // BLOCK)]
    load_v.wait()
    for at in blocks:
        out_ref[1, at, :] = raw_v_ref[at, :].T
    load_q.wait()
    for at in blocks:
        turned_ref[at, :] = raw_q_ref[at, :].T
    load_k.wait()


def bundle(queries, keys, values):
    rows = keys.shape[0]
    operands = [
        pltpu.with_memory_space_constraint(x, pltpu.MemorySpace.HBM)
        for x in (queries, keys, values)
    ]
    return pl.pallas_call(
        bundle_kernel,
        out_shape=(
            jax.ShapeDtypeStruct((2, rows, HEAD), keys.dtype),
            jax.ShapeDtypeStruct((rows, HEAD), queries.dtype),
        ),
        in_specs=[HBM] * 3,
        out_specs=[VMEM] * 2,
        scratch_shapes=[
            pltpu.VMEM((rows, HEAD), queries.dtype),
            pltpu.VMEM((rows, HEAD), values.dtype),
            pltpu.SemaphoreType.DMA((3,)),
        ],
        cost_estimate=cost(0, 4 * rows * HEAD * 2),
        compiler_params=grant(4),
        name="bundle",
    )(*operands)


def list_kernel(spots, own, allowed_ref, out_ref, rows_ref, sems):
    total = rows_ref.shape[1]
    pos = lax.axis_index("blk")
    core = lax.axis_index("node")
    side = pos % 2
    high = pos // 2
    levels = spots // 2
    mate = pos + 1 - 2 * side
    extra = pos - 1 + 2 * side
    extra_ok = (extra >= 0) & (extra < spots)
    first = high + 1 - 2 * (high % 2)
    second = high - 1 + 2 * (high % 2)
    first_ok = (first >= 0) & (first < levels)
    second_ok = (second >= 0) & (second < levels)
    far = high + 1 - 2 * side
    pair = 2 * own
    query_pairs = (pos, mate, jnp.where(extra_ok, extra, 0))
    copies = []
    for group, who in enumerate(query_pairs):
        begin = pl.multiple_of(who * pair + core * own, own)
        copies.append(
            pltpu.make_async_copy(
                allowed_ref.at[pl.ds(begin, own), :],
                rows_ref.at[pl.ds(group * own, own), :],
                sems.at[group],
            )
        )
    for copy in copies:
        copy.start()
    column = lax.broadcasted_iota(jnp.int32, (own, total), 1)
    inside = column % pair
    place = jnp.where(core == 0, inside, (inside + own) % pair)
    owner = column // pair
    none = jnp.int32(-1)
    one = jnp.where(first_ok, first * 2 + side, none)
    two = jnp.where(second_ok, second * 2 + side, none)
    one_x = jnp.where(first_ok & extra_ok & (first == far), one, none)
    two_x = jnp.where(second_ok & extra_ok & (second == far), two, none)
    near = (owner == pos).astype(jnp.int32)
    beside = ((owner == one) | (owner == two)).astype(jnp.int32)
    beyond = ((owner == one_x) | (owner == two_x)).astype(jnp.int32)
    later = (inside >= own) != (owner == two)
    value = place + jnp.where(later & (near == 0), pair, 0)
    ahead = (
        lax.broadcasted_iota(jnp.int32, (total, total), 0)
        < lax.broadcasted_iota(jnp.int32, (total, total), 1)
    ).astype(jnp.bfloat16)
    for copy in copies:
        copy.wait()
    lane = lax.broadcasted_iota(jnp.int32, (own, 128), 1)
    jobs = ((0, near, 1), (1, near, 1), (1, beside, 2), (0, beside, 2), (2, beyond, 2))
    for job, (group, wanted, widths) in enumerate(jobs):
        kept = (rows_ref[pl.ds(group * own, own), :] > 0).astype(jnp.int32) * wanted
        rank = lax.dot_general(
            kept.astype(jnp.bfloat16),
            ahead,
            (((1,), (0,)), ((), ())),
            preferred_element_type=jnp.float32,
        ).astype(jnp.int32)
        rank = jnp.where(kept > 0, rank, none)
        count = jnp.sum(kept, axis=1, keepdims=True)
        row = jnp.where(lane == COUNT_AT, count, 0)
        for t in range(widths * pair):
            found = jnp.sum(jnp.where(rank == t, value, 0), axis=1, keepdims=True)
            row = jnp.where(lane == t, found, row)
        out_ref[pl.ds(job * own, own), :] = row


def lists(allowed, own, spots):
    return pl.pallas_call(
        functools.partial(list_kernel, spots, own),
        out_shape=jax.ShapeDtypeStruct((5 * own, 128), jnp.int32),
        in_specs=[ANY],
        out_specs=VMEM,
        scratch_shapes=[
            pltpu.VMEM((3 * own, allowed.shape[1]), jnp.int32),
            pltpu.SemaphoreType.DMA((3,)),
        ],
        cost_estimate=cost(1000, 100000),
        compiler_params=grant(4 + allowed.shape[1] ** 2 // 2**16),
        name="lists",
    )(allowed)


def thirds(value):
    high = value.astype(jnp.bfloat16)
    rest = value - high.astype(jnp.float32)
    middle = rest.astype(jnp.bfloat16)
    low = (rest - middle.astype(jnp.float32)).astype(jnp.bfloat16)
    return high, middle, low


def packed_stats(ref, rows):
    own = rows // BLOCK
    pieces = [ref[pl.ds(rows + n * 2 * own, 2 * own), :].astype(jnp.float32) for n in range(3)]
    both = (pieces[2] + pieces[1]) + pieces[0]
    top, total = both[:own], both[own:]
    return jnp.where(total > 0, top, FLOOR), total


def attend_kernel(base, sources, resume, pack, table_ref, q_ref, *refs):
    rows = q_ref.shape[0]
    own = rows // BLOCK
    refs = list(refs)
    take = lambda count: [refs.pop(0) for _ in range(count)]
    source_refs = take(sources)
    if not sources:
        k_ref, v_ref = take(2)
    if resume:
        take(2)
    if pack:
        (out_ref,) = take(1)
    if sources:
        k_ref, v_ref = take(2)
    sum_ref, stat_ref, list_ref, sems = refs
    mine = table_ref.at[pl.ds(base, own), :]
    load_list = pltpu.make_async_copy(mine, list_ref, sems.at[2 * sources])
    load_list.start()
    copies = []
    for n, ref in enumerate(source_refs):
        at = pl.ds(n * rows, rows)
        copies.append(pltpu.make_async_copy(ref.at[0], k_ref.at[at, :], sems.at[2 * n]))
        copies.append(pltpu.make_async_copy(ref.at[1], v_ref.at[at, :], sems.at[2 * n + 1]))
    for copy in copies:
        copy.start()
    if not resume:
        sum_ref[...] = jnp.zeros_like(sum_ref)
        stat_ref[pl.ds(0, own), :] = jnp.full((own, BLOCK), FLOOR, jnp.float32)
        stat_ref[pl.ds(own, own), :] = jnp.zeros((own, BLOCK), jnp.float32)
    load_list.wait()
    counts = [list_ref[i, COUNT_AT] for i in range(own)]
    steps = counts[0]
    for count in counts[1:]:
        steps = jnp.maximum(steps, count)
    steps = (steps + WIDE - 1) // WIDE
    for copy in copies:
        copy.wait()
    tops = tuple(stat_ref[pl.ds(i, 1), :] for i in range(own))
    totals = tuple(stat_ref[pl.ds(own + i, 1), :] for i in range(own))

    def step(t, state):
        tops, totals = state
        new_tops, new_totals = [], []
        for i in range(own):
            mine = pl.ds(i * BLOCK, BLOCK)
            turned = q_ref[mine, :]
            spots, scores, biases = [], [], []
            top = tops[i]
            for u in range(WIDE):
                at = t * WIDE + u
                live = at < counts[i]
                index = jnp.where(live, list_ref[i, at], 0)
                bias = jnp.where(live, jnp.float32(0.0), jnp.float32(DROP))
                spot = pl.ds(pl.multiple_of(index * BLOCK, BLOCK), BLOCK)
                score = jnp.dot(k_ref[spot, :], turned, preferred_element_type=jnp.float32)
                top = jnp.maximum(top, jnp.max(score, axis=0, keepdims=True) + bias)
                spots.append(spot)
                scores.append(score)
                biases.append(bias)
            fade = jnp.exp2((tops[i] - top) * FACTOR)
            total, part = totals[i] * fade, None
            for spot, score, bias in zip(spots, scores, biases):
                weight = jnp.exp2((score + (bias - top)) * FACTOR)
                total = total + jnp.sum(weight, axis=0, keepdims=True)
                piece = jnp.dot(
                    v_ref[spot, :],
                    weight.astype(jnp.bfloat16),
                    preferred_element_type=jnp.float32,
                )
                part = piece if part is None else part + piece
            sum_ref[mine, :] = sum_ref[mine, :] * fade + part
            new_tops.append(top)
            new_totals.append(total)
        return tuple(new_tops), tuple(new_totals)

    tops, totals = lax.fori_loop(0, steps, step, (tops, totals))
    stats = jnp.concatenate(tops + totals, axis=0)
    if not pack:
        stat_ref[...] = stats
    else:
        for i in range(own):
            mine = pl.ds(i * BLOCK, BLOCK)
            inverse = 1.0 / jnp.maximum(totals[i], 1e-30)
            out_ref[mine, :] = (sum_ref[mine, :] * inverse).astype(jnp.bfloat16)
        for n, piece in enumerate(thirds(stats)):
            out_ref[pl.ds(rows + n * 2 * own, 2 * own), :] = piece
        spare = out_ref.shape[0] - rows - 6 * own
        if spare:
            out_ref[pl.ds(rows + 6 * own, spare), :] = jnp.zeros((spare, HEAD), out_ref.dtype)


def attend(job, table, queries, sources=(), gathered=(), state=(), pack=False, spare=0):
    rows = queries.shape[0]
    own = rows // BLOCK
    keys = len(sources) * rows if sources else gathered[0].shape[0]
    out_shape = []
    if pack:
        height = rows + 6 * own + 16 * spare
        out_shape.append(jax.ShapeDtypeStruct((height, HEAD), jnp.bfloat16))
    if sources:
        out_shape += [jax.ShapeDtypeStruct((keys, HEAD), queries.dtype)] * 2
    kept = [
        jax.ShapeDtypeStruct((rows, HEAD), jnp.float32),
        jax.ShapeDtypeStruct((2 * own, BLOCK), jnp.float32),
    ]
    scratch = []
    if pack and not state:
        scratch = [pltpu.VMEM(x.shape, x.dtype) for x in kept]
    else:
        out_shape += kept
    direct = [*gathered, *state]
    operands = 2 + len(sources) + len(direct)
    outs = len(out_shape)
    aliases = {operands - 2: outs - 2, operands - 1: outs - 1} if state else {}
    return pl.pallas_call(
        functools.partial(attend_kernel, job * own, len(sources), len(state) > 0, pack),
        out_shape=out_shape,
        in_specs=[ANY, VMEM] + [ANY] * len(sources) + [VMEM] * len(direct),
        out_specs=[VMEM] * outs,
        scratch_shapes=scratch
        + [
            pltpu.SMEM((own, table.shape[1]), jnp.int32),
            pltpu.SemaphoreType.DMA((2 * len(sources) + 1,)),
        ],
        input_output_aliases=aliases,
        cost_estimate=cost(1 << 20, 1 << 16),
        compiler_params=grant(8),
        name="attend%d" % job,
    )(table, queries, *sources, *direct)


def choose_kernel(one_ref, two_ref, out_ref):
    core = lax.axis_index("node")

    @pl.when(core == 0)
    def _():
        out_ref[...] = one_ref[...]

    @pl.when(core != 0)
    def _():
        out_ref[...] = two_ref[...]


def choose(one, two):
    return pl.pallas_call(
        choose_kernel,
        out_shape=jax.ShapeDtypeStruct(one.shape, one.dtype),
        in_specs=[VMEM] * 2,
        out_specs=VMEM,
        cost_estimate=cost(1 << 10, 1 << 10),
        compiler_params=grant(1),
        name="choose",
    )(one, two)


def merge_kernel(sum_ref, stat_ref, *refs):
    *other_refs, out_ref = refs
    rows = sum_ref.shape[0]
    own = rows // BLOCK
    top0, total0 = stat_ref[pl.ds(0, own), :], stat_ref[pl.ds(own, own), :]
    others = [packed_stats(ref, rows) for ref in other_refs]
    top = top0
    for their_top, _ in others:
        top = jnp.maximum(top, their_top)
    share = jnp.exp2((top0 - top) * FACTOR)
    shares = [jnp.exp2((a - top) * FACTOR) * b for a, b in others]
    inverse = 1.0 / sum(shares, share * total0)
    share = share * inverse
    shares = [x * inverse for x in shares]
    for i in range(own):
        mine = pl.ds(i * BLOCK, BLOCK)
        row = slice(i, i + 1)
        mixed = sum_ref[mine, :] * share[row]
        for ref, part in zip(other_refs, shares):
            mixed = mixed + ref[mine, :].astype(jnp.float32) * part[row]
        out_ref[mine, :] = mixed.astype(jnp.bfloat16).T


def merge(state, *others):
    rows = state[0].shape[0]
    return pl.pallas_call(
        merge_kernel,
        out_shape=jax.ShapeDtypeStruct((rows, HEAD), jnp.bfloat16),
        in_specs=[VMEM] * (2 + len(others)),
        out_specs=VMEM,
        cost_estimate=cost(8 * rows * HEAD, 10 * rows * HEAD),
        compiler_params=grant(4),
        name="merge",
    )(*state, *others)


def shards(queries, keys, values, allowed):
    rows = queries.shape[0]
    own = rows // BLOCK
    spots = lax.axis_size("blk")
    levels = spots // 2

    def hop(value, target):
        pairs = []
        for i in range(spots):
            high, side = target(i // 2, i % 2)
            if 0 <= high < levels:
                pairs.append((i, high * 2 + side))
        return lax.ppermute(value, "blk", pairs)

    def across(value):
        return hop(value, lambda high, side: (high, 1 - side))

    def swap(value):
        return lax.ppermute(value, "node", [(0, 1), (1, 0)])

    def trade(value, turn):
        pairs = []
        for i in range(spots):
            high, side = i // 2, i % 2
            for core in range(2):
                far = (high ^ 1) if core == turn else ((high + 1) ^ 1) - 1
                if 0 <= far < levels:
                    pairs.append((2 * i + core, 2 * (far * 2 + side) + core))
        return lax.ppermute(value, ("blk", "node"), pairs)

    def visit(value):
        pairs = []
        for i in range(spots):
            high, side = i // 2, i % 2
            for core in range(2):
                came = side if core == 0 else 1 - side
                far = high + 1 - 2 * came
                if 0 < far < levels - 1:
                    pairs.append((2 * i + core, 2 * (far * 2 + came) + core))
        return lax.ppermute(value, ("blk", "node"), pairs)

    tie = lax.optimization_barrier
    bundled, turned = bundle(queries, keys, values)
    mates = across(turned)
    first = trade(bundled, 0)
    second = trade(bundled, 1)
    other = swap(bundled)
    table = lists(allowed, own, spots)
    *near, sums, stats = attend(0, table, turned, (bundled, other))
    mate_state = attend(1, table, mates, gathered=near)
    parcel = choose(mates, turned)
    first, second, mates, mate_state = tie((first, second, mates, mate_state))
    guests = visit(parcel)
    beside = (first, swap(first), second, swap(second))
    mate_part, *beside, _, _ = attend(2, table, mates, beside, state=mate_state, pack=True, spare=2)
    one = across(mate_part)
    state = attend(3, table, turned, gathered=beside, state=(sums, stats))
    (guest_part,) = attend(4, table, guests, gathered=beside, pack=True)
    homeward = []
    for i in range(2, spots - 2):
        high, side = i // 2, i % 2
        homeward.append((i, (high - 1 + 2 * side) * 2 + 1 - side))
    two = lax.ppermute(guest_part, "blk", homeward)
    return merge(state, one, two)


def solution(mesh):
    placed = (
        P(("grp", "blk", "node"), None),
        P(("grp", "blk", "node"), None),
        P(("grp", "blk", "node"), None),
        P("grp", None),
    )
    return jax.shard_map(
        shards,
        mesh=mesh,
        in_specs=placed,
        out_specs=P(("grp", "blk", "node"), None),
        check_vma=False,
    )
```

```python
import functools
import math

import jax
import jax.numpy as jnp
from jax import lax
from jax.experimental import pallas as pl
from jax.experimental.pallas import tpu as pltpu
from jax.sharding import PartitionSpec as P

HEAD = 128
BLOCK = 128
FLOOR = -1e30
DROP = -3e38
FACTOR = HEAD ** (-0.5) * math.log2(math.e)
COUNT_AT = 64
WIDTHS = (4, 4, 5, 4, 4)

ANY = pl.BlockSpec(memory_space=pl.ANY)
HBM = pl.BlockSpec(memory_space=pltpu.HBM)
VMEM = pl.BlockSpec(memory_space=pltpu.VMEM)


def cost(flops, moved, exps=0):
    return pl.CostEstimate(flops=flops, bytes_accessed=moved, transcendentals=exps)


def grant(size):
    return pltpu.CompilerParams(vmem_limit_bytes=size << 20)


def bundle_kernel(q_ref, k_ref, v_ref, out_ref, turned_ref, raw_q_ref, raw_v_ref, sems):
    load_v = pltpu.make_async_copy(v_ref, raw_v_ref, sems.at[0])
    load_k = pltpu.make_async_copy(k_ref, out_ref.at[0], sems.at[1])
    load_q = pltpu.make_async_copy(q_ref, raw_q_ref, sems.at[2])
    load_v.start()
    load_k.start()
    load_q.start()
    blocks = [pl.ds(n * BLOCK, BLOCK) for n in range(raw_v_ref.shape[0] // BLOCK)]
    load_v.wait()
    for at in blocks:
        out_ref[1, at, :] = raw_v_ref[at, :].T
    load_q.wait()
    for at in blocks:
        turned_ref[at, :] = raw_q_ref[at, :].T
    load_k.wait()


def bundle(queries, keys, values):
    rows = keys.shape[0]
    operands = [
        pltpu.with_memory_space_constraint(x, pltpu.MemorySpace.HBM)
        for x in (queries, keys, values)
    ]
    return pl.pallas_call(
        bundle_kernel,
        out_shape=(
            jax.ShapeDtypeStruct((2, rows, HEAD), keys.dtype),
            jax.ShapeDtypeStruct((rows, HEAD), queries.dtype),
        ),
        in_specs=[HBM] * 3,
        out_specs=[VMEM] * 2,
        scratch_shapes=[
            pltpu.VMEM((rows, HEAD), queries.dtype),
            pltpu.VMEM((rows, HEAD), values.dtype),
            pltpu.SemaphoreType.DMA((3,)),
        ],
        cost_estimate=cost(0, 4 * rows * HEAD * 2),
        compiler_params=grant(4),
        name="bundle",
    )(*operands)


def list_kernel(spots, own, allowed_ref, out_ref, rows_ref, sems):
    total = rows_ref.shape[1]
    pos = lax.axis_index("blk")
    core = lax.axis_index("node")
    side = pos % 2
    high = pos // 2
    levels = spots // 2
    mate = pos + 1 - 2 * side
    extra = pos - 1 + 2 * side
    extra_ok = (extra >= 0) & (extra < spots)
    first = high + 1 - 2 * (high % 2)
    second = high - 1 + 2 * (high % 2)
    first_ok = (first >= 0) & (first < levels)
    second_ok = (second >= 0) & (second < levels)
    far = high + 1 - 2 * side
    pair = 2 * own
    query_pairs = (pos, mate, jnp.where(extra_ok, extra, 0))
    copies = []
    for group, who in enumerate(query_pairs):
        begin = pl.multiple_of(who * pair + core * own, own)
        copies.append(
            pltpu.make_async_copy(
                allowed_ref.at[pl.ds(begin, own), :],
                rows_ref.at[pl.ds(group * own, own), :],
                sems.at[group],
            )
        )
    for copy in copies:
        copy.start()
    column = lax.broadcasted_iota(jnp.int32, (own, total), 1)
    inside = column % pair
    place = jnp.where(core == 0, inside, (inside + own) % pair)
    owner = column // pair
    none = jnp.int32(-1)
    one = jnp.where(first_ok, first * 2 + side, none)
    two = jnp.where(second_ok, second * 2 + side, none)
    one_x = jnp.where(first_ok & extra_ok & (first == far), one, none)
    two_x = jnp.where(second_ok & extra_ok & (second == far), two, none)
    near = (owner == pos).astype(jnp.int32)
    beside = ((owner == one) | (owner == two)).astype(jnp.int32)
    beyond = ((owner == one_x) | (owner == two_x)).astype(jnp.int32)
    later = (inside >= own) != (owner == two)
    value = place + jnp.where(later & (near == 0), pair, 0)
    ahead = (
        lax.broadcasted_iota(jnp.int32, (total, total), 0)
        < lax.broadcasted_iota(jnp.int32, (total, total), 1)
    ).astype(jnp.bfloat16)
    for copy in copies:
        copy.wait()
    lane = lax.broadcasted_iota(jnp.int32, (own, 128), 1)
    jobs = ((0, near, 1), (1, near, 1), (1, beside, 2), (0, beside, 2), (2, beyond, 2))
    for job, (group, wanted, widths) in enumerate(jobs):
        kept = (rows_ref[pl.ds(group * own, own), :] > 0).astype(jnp.int32) * wanted
        rank = lax.dot_general(
            kept.astype(jnp.bfloat16),
            ahead,
            (((1,), (0,)), ((), ())),
            preferred_element_type=jnp.float32,
        ).astype(jnp.int32)
        rank = jnp.where(kept > 0, rank, none)
        count = jnp.sum(kept, axis=1, keepdims=True)
        row = jnp.where(lane == COUNT_AT, count, 0)
        for t in range(widths * pair):
            found = jnp.sum(jnp.where(rank == t, value, 0), axis=1, keepdims=True)
            row = jnp.where(lane == t, found, row)
        out_ref[pl.ds(job * own, own), :] = row


def lists(allowed, own, spots):
    return pl.pallas_call(
        functools.partial(list_kernel, spots, own),
        out_shape=jax.ShapeDtypeStruct((5 * own, 128), jnp.int32),
        in_specs=[ANY],
        out_specs=VMEM,
        scratch_shapes=[
            pltpu.VMEM((3 * own, allowed.shape[1]), jnp.int32),
            pltpu.SemaphoreType.DMA((3,)),
        ],
        cost_estimate=cost(1000, 100000),
        compiler_params=grant(4 + allowed.shape[1] ** 2 // 2**16),
        name="lists",
    )(allowed)


def thirds(value):
    high = value.astype(jnp.bfloat16)
    rest = value - high.astype(jnp.float32)
    middle = rest.astype(jnp.bfloat16)
    low = (rest - middle.astype(jnp.float32)).astype(jnp.bfloat16)
    return high, middle, low


def packed_stats(ref, rows):
    own = rows // BLOCK
    pieces = [ref[pl.ds(rows + n * 2 * own, 2 * own), :].astype(jnp.float32) for n in range(3)]
    both = (pieces[2] + pieces[1]) + pieces[0]
    top, total = both[:own], both[own:]
    return jnp.where(total > 0, top, FLOOR), total


def attend_kernel(base, wide, sources, resume, pack, table_ref, q_ref, *refs):
    rows = q_ref.shape[0]
    own = rows // BLOCK
    refs = list(refs)
    take = lambda count: [refs.pop(0) for _ in range(count)]
    source_refs = take(sources)
    if not sources:
        k_ref, v_ref = take(2)
    if resume:
        take(2)
    if pack:
        (out_ref,) = take(1)
    if sources:
        k_ref, v_ref = take(2)
    sum_ref, stat_ref, list_ref, sems = refs
    mine = table_ref.at[pl.ds(base, own), :]
    load_list = pltpu.make_async_copy(mine, list_ref, sems.at[2 * sources])
    load_list.start()
    copies = []
    for n, ref in enumerate(source_refs):
        at = pl.ds(n * rows, rows)
        copies.append(pltpu.make_async_copy(ref.at[0], k_ref.at[at, :], sems.at[2 * n]))
        copies.append(pltpu.make_async_copy(ref.at[1], v_ref.at[at, :], sems.at[2 * n + 1]))
    for copy in copies:
        copy.start()
    if not resume:
        sum_ref[...] = jnp.zeros_like(sum_ref)
        stat_ref[pl.ds(0, own), :] = jnp.full((own, BLOCK), FLOOR, jnp.float32)
        stat_ref[pl.ds(own, own), :] = jnp.zeros((own, BLOCK), jnp.float32)
    load_list.wait()
    counts = [list_ref[i, COUNT_AT] for i in range(own)]
    steps = counts[0]
    for count in counts[1:]:
        steps = jnp.maximum(steps, count)
    steps = (steps + wide - 1) // wide
    for copy in copies:
        copy.wait()
    tops = tuple(stat_ref[pl.ds(i, 1), :] for i in range(own))
    totals = tuple(stat_ref[pl.ds(own + i, 1), :] for i in range(own))

    def step(t, state):
        tops, totals = state
        new_tops, new_totals = [], []
        for i in range(own):
            mine = pl.ds(i * BLOCK, BLOCK)
            turned = q_ref[mine, :]
            spots, scores, biases = [], [], []
            top = tops[i]
            for u in range(wide):
                at = t * wide + u
                live = at < counts[i]
                index = jnp.where(live, list_ref[i, at], 0)
                bias = jnp.where(live, jnp.float32(0.0), jnp.float32(DROP))
                spot = pl.ds(pl.multiple_of(index * BLOCK, BLOCK), BLOCK)
                score = jnp.dot(k_ref[spot, :], turned, preferred_element_type=jnp.float32)
                top = jnp.maximum(top, jnp.max(score, axis=0, keepdims=True) + bias)
                spots.append(spot)
                scores.append(score)
                biases.append(bias)
            fade = jnp.exp2((tops[i] - top) * FACTOR)
            total, part = totals[i] * fade, None
            for spot, score, bias in zip(spots, scores, biases):
                weight = jnp.exp2((score + (bias - top)) * FACTOR)
                total = total + jnp.sum(weight, axis=0, keepdims=True)
                piece = jnp.dot(
                    v_ref[spot, :],
                    weight.astype(jnp.bfloat16),
                    preferred_element_type=jnp.float32,
                )
                part = piece if part is None else part + piece
            sum_ref[mine, :] = sum_ref[mine, :] * fade + part
            new_tops.append(top)
            new_totals.append(total)
        return tuple(new_tops), tuple(new_totals)

    tops, totals = lax.fori_loop(0, steps, step, (tops, totals))
    stats = jnp.concatenate(tops + totals, axis=0)
    if not pack:
        stat_ref[...] = stats
    else:
        for i in range(own):
            mine = pl.ds(i * BLOCK, BLOCK)
            inverse = 1.0 / jnp.maximum(totals[i], 1e-30)
            out_ref[mine, :] = (sum_ref[mine, :] * inverse).astype(jnp.bfloat16)
        for n, piece in enumerate(thirds(stats)):
            out_ref[pl.ds(rows + n * 2 * own, 2 * own), :] = piece
        spare = out_ref.shape[0] - rows - 6 * own
        if spare:
            out_ref[pl.ds(rows + 6 * own, spare), :] = jnp.zeros((spare, HEAD), out_ref.dtype)


def attend(job, table, queries, sources=(), gathered=(), state=(), pack=False, spare=0):
    rows = queries.shape[0]
    own = rows // BLOCK
    keys = len(sources) * rows if sources else gathered[0].shape[0]
    out_shape = []
    if pack:
        height = rows + 6 * own + 16 * spare
        out_shape.append(jax.ShapeDtypeStruct((height, HEAD), jnp.bfloat16))
    if sources:
        out_shape += [jax.ShapeDtypeStruct((keys, HEAD), queries.dtype)] * 2
    kept = [
        jax.ShapeDtypeStruct((rows, HEAD), jnp.float32),
        jax.ShapeDtypeStruct((2 * own, BLOCK), jnp.float32),
    ]
    scratch = []
    if pack and not state:
        scratch = [pltpu.VMEM(x.shape, x.dtype) for x in kept]
    else:
        out_shape += kept
    direct = [*gathered, *state]
    operands = 2 + len(sources) + len(direct)
    outs = len(out_shape)
    aliases = {operands - 2: outs - 2, operands - 1: outs - 1} if state else {}
    return pl.pallas_call(
        functools.partial(attend_kernel, job * own, WIDTHS[job], len(sources), len(state) > 0, pack),
        out_shape=out_shape,
        in_specs=[ANY, VMEM] + [ANY] * len(sources) + [VMEM] * len(direct),
        out_specs=[VMEM] * outs,
        scratch_shapes=scratch
        + [
            pltpu.SMEM((own, table.shape[1]), jnp.int32),
            pltpu.SemaphoreType.DMA((2 * len(sources) + 1,)),
        ],
        input_output_aliases=aliases,
        cost_estimate=cost(1 << 20, 1 << 16),
        compiler_params=grant(8),
        name="attend%d" % job,
    )(table, queries, *sources, *direct)


def choose_kernel(one_ref, two_ref, out_ref):
    core = lax.axis_index("node")

    @pl.when(core == 0)
    def _():
        out_ref[...] = one_ref[...]

    @pl.when(core != 0)
    def _():
        out_ref[...] = two_ref[...]


def choose(one, two):
    return pl.pallas_call(
        choose_kernel,
        out_shape=jax.ShapeDtypeStruct(one.shape, one.dtype),
        in_specs=[VMEM] * 2,
        out_specs=VMEM,
        cost_estimate=cost(1 << 10, 1 << 10),
        compiler_params=grant(1),
        name="choose",
    )(one, two)


def merge_kernel(sum_ref, stat_ref, *refs):
    *other_refs, out_ref, done_ref, sems = refs
    rows = sum_ref.shape[0]
    own = rows // BLOCK
    top0, total0 = stat_ref[pl.ds(0, own), :], stat_ref[pl.ds(own, own), :]
    others = [packed_stats(ref, rows) for ref in other_refs]
    top = top0
    for their_top, _ in others:
        top = jnp.maximum(top, their_top)
    share = jnp.exp2((top0 - top) * FACTOR)
    shares = [jnp.exp2((a - top) * FACTOR) * b for a, b in others]
    inverse = 1.0 / sum(shares, share * total0)
    share = share * inverse
    shares = [x * inverse for x in shares]
    copies = []
    for i in range(own):
        mine = pl.ds(i * BLOCK, BLOCK)
        row = slice(i, i + 1)
        mixed = sum_ref[mine, :] * share[row]
        for ref, part in zip(other_refs, shares):
            mixed = mixed + ref[mine, :].astype(jnp.float32) * part[row]
        done_ref[mine, :] = mixed.astype(jnp.bfloat16).T
        copy = pltpu.make_async_copy(done_ref.at[mine, :], out_ref.at[mine, :], sems.at[i])
        copy.start()
        copies.append(copy)
    for copy in copies:
        copy.wait()


def merge(state, *others):
    rows = state[0].shape[0]
    return pl.pallas_call(
        merge_kernel,
        out_shape=jax.ShapeDtypeStruct((rows, HEAD), jnp.bfloat16),
        in_specs=[VMEM] * (2 + len(others)),
        out_specs=ANY,
        scratch_shapes=[
            pltpu.VMEM((rows, HEAD), jnp.bfloat16),
            pltpu.SemaphoreType.DMA((rows // BLOCK,)),
        ],
        cost_estimate=cost(8 * rows * HEAD, 10 * rows * HEAD),
        compiler_params=grant(4),
        name="merge",
    )(*state, *others)


def shards(queries, keys, values, allowed):
    rows = queries.shape[0]
    own = rows // BLOCK
    spots = lax.axis_size("blk")
    levels = spots // 2

    def hop(value, target):
        pairs = []
        for i in range(spots):
            high, side = target(i // 2, i % 2)
            if 0 <= high < levels:
                pairs.append((i, high * 2 + side))
        return lax.ppermute(value, "blk", pairs)

    def across(value):
        return hop(value, lambda high, side: (high, 1 - side))

    def swap(value):
        return lax.ppermute(value, "node", [(0, 1), (1, 0)])

    def trade(value, turn):
        pairs = []
        for i in range(spots):
            high, side = i // 2, i % 2
            for core in range(2):
                far = (high ^ 1) if core == turn else ((high + 1) ^ 1) - 1
                if 0 <= far < levels:
                    pairs.append((2 * i + core, 2 * (far * 2 + side) + core))
        return lax.ppermute(value, ("blk", "node"), pairs)

    def visit(value):
        pairs = []
        for i in range(spots):
            high, side = i // 2, i % 2
            for core in range(2):
                came = side if core == 0 else 1 - side
                far = high + 1 - 2 * came
                if 0 < far < levels - 1:
                    pairs.append((2 * i + core, 2 * (far * 2 + came) + core))
        return lax.ppermute(value, ("blk", "node"), pairs)

    tie = lax.optimization_barrier
    bundled, turned = bundle(queries, keys, values)
    mates = across(turned)
    first = trade(bundled, 0)
    second = trade(bundled, 1)
    other = swap(bundled)
    table = lists(allowed, own, spots)
    *near, sums, stats = attend(0, table, turned, (bundled, other))
    mate_state = attend(1, table, mates, gathered=near)
    parcel = choose(mates, turned)
    first, second, mates, mate_state = tie((first, second, mates, mate_state))
    guests = visit(parcel)
    beside = (first, swap(first), second, swap(second))
    mate_part, *beside, _, _ = attend(2, table, mates, beside, state=mate_state, pack=True, spare=2)
    one = across(mate_part)
    state = attend(3, table, turned, gathered=beside, state=(sums, stats))
    (guest_part,) = attend(4, table, guests, gathered=beside, pack=True)
    homeward = []
    for i in range(2, spots - 2):
        high, side = i // 2, i % 2
        homeward.append((i, (high - 1 + 2 * side) * 2 + 1 - side))
    two = lax.ppermute(guest_part, "blk", homeward)
    return merge(state, one, two)


def solution(mesh):
    placed = (
        P(("grp", "blk", "node"), None),
        P(("grp", "blk", "node"), None),
        P(("grp", "blk", "node"), None),
        P("grp", None),
    )
    return jax.shard_map(
        shards,
        mesh=mesh,
        in_specs=placed,
        out_specs=P(("grp", "blk", "node"), None),
        check_vma=False,
    )
```

```python
import functools
import math

import jax
import jax.numpy as jnp
from jax import lax
from jax.experimental import pallas as pl
from jax.experimental.pallas import tpu as pltpu
from jax.sharding import PartitionSpec as P

HEAD = 128
BLOCK = 128
FLOOR = -1e30
DROP = -3e38
FACTOR = HEAD ** (-0.5) * math.log2(math.e)
COUNT_AT = 64
WIDTHS = (4, 4, 4, 4, 3)

ANY = pl.BlockSpec(memory_space=pl.ANY)
HBM = pl.BlockSpec(memory_space=pltpu.HBM)
VMEM = pl.BlockSpec(memory_space=pltpu.VMEM)


def cost(flops, moved, exps=0):
    return pl.CostEstimate(flops=flops, bytes_accessed=moved, transcendentals=exps)


def grant(size):
    return pltpu.CompilerParams(vmem_limit_bytes=size << 20)


def bundle_kernel(q_ref, k_ref, v_ref, out_ref, turned_ref, raw_q_ref, raw_v_ref, sems):
    load_v = pltpu.make_async_copy(v_ref, raw_v_ref, sems.at[0])
    load_k = pltpu.make_async_copy(k_ref, out_ref.at[0], sems.at[1])
    load_q = pltpu.make_async_copy(q_ref, raw_q_ref, sems.at[2])
    load_v.start()
    load_k.start()
    load_q.start()
    blocks = [pl.ds(n * BLOCK, BLOCK) for n in range(raw_v_ref.shape[0] // BLOCK)]
    load_v.wait()
    for at in blocks:
        out_ref[1, at, :] = raw_v_ref[at, :].T
    load_q.wait()
    for at in blocks:
        turned_ref[at, :] = raw_q_ref[at, :].T
    load_k.wait()


def bundle(queries, keys, values):
    rows = keys.shape[0]
    operands = [
        pltpu.with_memory_space_constraint(x, pltpu.MemorySpace.HBM)
        for x in (queries, keys, values)
    ]
    return pl.pallas_call(
        bundle_kernel,
        out_shape=(
            jax.ShapeDtypeStruct((2, rows, HEAD), keys.dtype),
            jax.ShapeDtypeStruct((rows, HEAD), queries.dtype),
        ),
        in_specs=[HBM] * 3,
        out_specs=[VMEM] * 2,
        scratch_shapes=[
            pltpu.VMEM((rows, HEAD), queries.dtype),
            pltpu.VMEM((rows, HEAD), values.dtype),
            pltpu.SemaphoreType.DMA((3,)),
        ],
        cost_estimate=cost(0, 4 * rows * HEAD * 2),
        compiler_params=grant(4),
        name="bundle",
    )(*operands)


def list_kernel(spots, own, allowed_ref, out_ref, rows_ref, sems):
    total = rows_ref.shape[1]
    pos = lax.axis_index("blk")
    core = lax.axis_index("node")
    side = pos % 2
    high = pos // 2
    levels = spots // 2
    mate = pos + 1 - 2 * side
    extra = pos - 1 + 2 * side
    extra_ok = (extra >= 0) & (extra < spots)
    first = high + 1 - 2 * (high % 2)
    second = high - 1 + 2 * (high % 2)
    first_ok = (first >= 0) & (first < levels)
    second_ok = (second >= 0) & (second < levels)
    far = high + 1 - 2 * side
    pair = 2 * own
    query_pairs = (pos, mate, jnp.where(extra_ok, extra, 0))
    copies = []
    for group, who in enumerate(query_pairs):
        begin = pl.multiple_of(who * pair + core * own, own)
        copies.append(
            pltpu.make_async_copy(
                allowed_ref.at[pl.ds(begin, own), :],
                rows_ref.at[pl.ds(group * own, own), :],
                sems.at[group],
            )
        )
    for copy in copies:
        copy.start()
    column = lax.broadcasted_iota(jnp.int32, (own, total), 1)
    inside = column % pair
    place = jnp.where(core == 0, inside, (inside + own) % pair)
    owner = column // pair
    none = jnp.int32(-1)
    one = jnp.where(first_ok, first * 2 + side, none)
    two = jnp.where(second_ok, second * 2 + side, none)
    one_x = jnp.where(first_ok & extra_ok & (first == far), one, none)
    two_x = jnp.where(second_ok & extra_ok & (second == far), two, none)
    near = (owner == pos).astype(jnp.int32)
    beside = ((owner == one) | (owner == two)).astype(jnp.int32)
    beyond = ((owner == one_x) | (owner == two_x)).astype(jnp.int32)
    later = (inside >= own) != (owner == two)
    value = place + jnp.where(later & (near == 0), pair, 0)
    ahead = (
        lax.broadcasted_iota(jnp.int32, (total, total), 0)
        < lax.broadcasted_iota(jnp.int32, (total, total), 1)
    ).astype(jnp.bfloat16)
    for copy in copies:
        copy.wait()
    lane = lax.broadcasted_iota(jnp.int32, (own, 128), 1)
    jobs = ((0, near, 1), (1, near, 1), (1, beside, 2), (0, beside, 2), (2, beyond, 2))
    for job, (group, wanted, widths) in enumerate(jobs):
        kept = (rows_ref[pl.ds(group * own, own), :] > 0).astype(jnp.int32) * wanted
        rank = lax.dot_general(
            kept.astype(jnp.bfloat16),
            ahead,
            (((1,), (0,)), ((), ())),
            preferred_element_type=jnp.float32,
        ).astype(jnp.int32)
        rank = jnp.where(kept > 0, rank, none)
        count = jnp.sum(kept, axis=1, keepdims=True)
        row = jnp.where(lane == COUNT_AT, count, 0)
        for t in range(widths * pair):
            found = jnp.sum(jnp.where(rank == t, value, 0), axis=1, keepdims=True)
            row = jnp.where(lane == t, found, row)
        out_ref[pl.ds(job * own, own), :] = row


def lists(allowed, own, spots):
    return pl.pallas_call(
        functools.partial(list_kernel, spots, own),
        out_shape=jax.ShapeDtypeStruct((5 * own, 128), jnp.int32),
        in_specs=[ANY],
        out_specs=VMEM,
        scratch_shapes=[
            pltpu.VMEM((3 * own, allowed.shape[1]), jnp.int32),
            pltpu.SemaphoreType.DMA((3,)),
        ],
        cost_estimate=cost(1000, 100000),
        compiler_params=grant(4 + allowed.shape[1] ** 2 // 2**16),
        name="lists",
    )(allowed)


def thirds(value):
    high = value.astype(jnp.bfloat16)
    rest = value - high.astype(jnp.float32)
    middle = rest.astype(jnp.bfloat16)
    low = (rest - middle.astype(jnp.float32)).astype(jnp.bfloat16)
    return high, middle, low


def packed_stats(ref, rows):
    own = rows // BLOCK
    pieces = [ref[pl.ds(rows + n * 2 * own, 2 * own), :].astype(jnp.float32) for n in range(3)]
    both = (pieces[2] + pieces[1]) + pieces[0]
    top, total = both[:own], both[own:]
    return jnp.where(total > 0, top, FLOOR), total


def attend_kernel(base, wide, sources, resume, pack, table_ref, q_ref, *refs):
    rows = q_ref.shape[0]
    own = rows // BLOCK
    refs = list(refs)
    take = lambda count: [refs.pop(0) for _ in range(count)]
    source_refs = take(sources)
    if not sources:
        k_ref, v_ref = take(2)
    if resume:
        take(2)
    if pack:
        (out_ref,) = take(1)
    if sources:
        k_ref, v_ref = take(2)
    sum_ref, stat_ref, list_ref, sems = refs
    mine = table_ref.at[pl.ds(base, own), :]
    load_list = pltpu.make_async_copy(mine, list_ref, sems.at[2 * sources])
    load_list.start()
    copies = []
    for n, ref in enumerate(source_refs):
        at = pl.ds(n * rows, rows)
        copies.append(pltpu.make_async_copy(ref.at[0], k_ref.at[at, :], sems.at[2 * n]))
        copies.append(pltpu.make_async_copy(ref.at[1], v_ref.at[at, :], sems.at[2 * n + 1]))
    for copy in copies:
        copy.start()
    if not resume:
        sum_ref[...] = jnp.zeros_like(sum_ref)
        stat_ref[pl.ds(0, own), :] = jnp.full((own, BLOCK), FLOOR, jnp.float32)
        stat_ref[pl.ds(own, own), :] = jnp.zeros((own, BLOCK), jnp.float32)
    load_list.wait()
    counts = [list_ref[i, COUNT_AT] for i in range(own)]
    steps = counts[0]
    for count in counts[1:]:
        steps = jnp.maximum(steps, count)
    steps = (steps + wide - 1) // wide
    for copy in copies:
        copy.wait()
    tops = tuple(stat_ref[pl.ds(i, 1), :] for i in range(own))
    totals = tuple(stat_ref[pl.ds(own + i, 1), :] for i in range(own))

    def step(t, state):
        tops, totals = state
        new_tops, new_totals = [], []
        for i in range(own):
            mine = pl.ds(i * BLOCK, BLOCK)
            turned = q_ref[mine, :]
            spots, scores, biases = [], [], []
            top = tops[i]
            for u in range(wide):
                at = t * wide + u
                live = at < counts[i]
                index = jnp.where(live, list_ref[i, at], 0)
                bias = jnp.where(live, jnp.float32(0.0), jnp.float32(DROP))
                spot = pl.ds(pl.multiple_of(index * BLOCK, BLOCK), BLOCK)
                score = jnp.dot(k_ref[spot, :], turned, preferred_element_type=jnp.float32)
                top = jnp.maximum(top, jnp.max(score, axis=0, keepdims=True) + bias)
                spots.append(spot)
                scores.append(score)
                biases.append(bias)
            fade = jnp.exp2((tops[i] - top) * FACTOR)
            total, part = totals[i] * fade, None
            for spot, score, bias in zip(spots, scores, biases):
                weight = jnp.exp2((score + (bias - top)) * FACTOR)
                total = total + jnp.sum(weight, axis=0, keepdims=True)
                piece = jnp.dot(
                    v_ref[spot, :],
                    weight.astype(jnp.bfloat16),
                    preferred_element_type=jnp.float32,
                )
                part = piece if part is None else part + piece
            sum_ref[mine, :] = sum_ref[mine, :] * fade + part
            new_tops.append(top)
            new_totals.append(total)
        return tuple(new_tops), tuple(new_totals)

    tops, totals = lax.fori_loop(0, steps, step, (tops, totals))
    stats = jnp.concatenate(tops + totals, axis=0)
    if not pack:
        stat_ref[...] = stats
    else:
        for i in range(own):
            mine = pl.ds(i * BLOCK, BLOCK)
            inverse = 1.0 / jnp.maximum(totals[i], 1e-30)
            out_ref[mine, :] = (sum_ref[mine, :] * inverse).astype(jnp.bfloat16)
        for n, piece in enumerate(thirds(stats)):
            out_ref[pl.ds(rows + n * 2 * own, 2 * own), :] = piece
        spare = out_ref.shape[0] - rows - 6 * own
        if spare:
            out_ref[pl.ds(rows + 6 * own, spare), :] = jnp.zeros((spare, HEAD), out_ref.dtype)


def attend(job, table, queries, sources=(), gathered=(), state=(), pack=False, spare=0):
    rows = queries.shape[0]
    own = rows // BLOCK
    keys = len(sources) * rows if sources else gathered[0].shape[0]
    out_shape = []
    if pack:
        height = rows + 6 * own + 16 * spare
        out_shape.append(jax.ShapeDtypeStruct((height, HEAD), jnp.bfloat16))
    if sources:
        out_shape += [jax.ShapeDtypeStruct((keys, HEAD), queries.dtype)] * 2
    kept = [
        jax.ShapeDtypeStruct((rows, HEAD), jnp.float32),
        jax.ShapeDtypeStruct((2 * own, BLOCK), jnp.float32),
    ]
    scratch = []
    if pack and not state:
        scratch = [pltpu.VMEM(x.shape, x.dtype) for x in kept]
    else:
        out_shape += kept
    direct = [*gathered, *state]
    operands = 2 + len(sources) + len(direct)
    outs = len(out_shape)
    aliases = {operands - 2: outs - 2, operands - 1: outs - 1} if state else {}
    return pl.pallas_call(
        functools.partial(attend_kernel, job * own, WIDTHS[job], len(sources), len(state) > 0, pack),
        out_shape=out_shape,
        in_specs=[ANY, VMEM] + [ANY] * len(sources) + [VMEM] * len(direct),
        out_specs=[VMEM] * outs,
        scratch_shapes=scratch
        + [
            pltpu.SMEM((own, table.shape[1]), jnp.int32),
            pltpu.SemaphoreType.DMA((2 * len(sources) + 1,)),
        ],
        input_output_aliases=aliases,
        cost_estimate=cost(1 << 20, 1 << 16),
        compiler_params=grant(8),
        name="attend%d" % job,
    )(table, queries, *sources, *direct)


def choose_kernel(one_ref, two_ref, out_ref):
    core = lax.axis_index("node")

    @pl.when(core == 0)
    def _():
        out_ref[...] = one_ref[...]

    @pl.when(core != 0)
    def _():
        out_ref[...] = two_ref[...]


def choose(one, two):
    return pl.pallas_call(
        choose_kernel,
        out_shape=jax.ShapeDtypeStruct(one.shape, one.dtype),
        in_specs=[VMEM] * 2,
        out_specs=VMEM,
        cost_estimate=cost(1 << 10, 1 << 10),
        compiler_params=grant(1),
        name="choose",
    )(one, two)


def merge_kernel(sum_ref, stat_ref, *refs):
    *other_refs, out_ref, done_ref, sems = refs
    rows = sum_ref.shape[0]
    own = rows // BLOCK
    top0, total0 = stat_ref[pl.ds(0, own), :], stat_ref[pl.ds(own, own), :]
    others = [packed_stats(ref, rows) for ref in other_refs]
    top = top0
    for their_top, _ in others:
        top = jnp.maximum(top, their_top)
    share = jnp.exp2((top0 - top) * FACTOR)
    shares = [jnp.exp2((a - top) * FACTOR) * b for a, b in others]
    inverse = 1.0 / sum(shares, share * total0)
    share = share * inverse
    shares = [x * inverse for x in shares]
    copies = []
    for i in range(own):
        mine = pl.ds(i * BLOCK, BLOCK)
        row = slice(i, i + 1)
        mixed = sum_ref[mine, :] * share[row]
        for ref, part in zip(other_refs, shares):
            mixed = mixed + ref[mine, :].astype(jnp.float32) * part[row]
        done_ref[mine, :] = mixed.astype(jnp.bfloat16).T
        copy = pltpu.make_async_copy(done_ref.at[mine, :], out_ref.at[mine, :], sems.at[i])
        copy.start()
        copies.append(copy)
    for copy in copies:
        copy.wait()


def merge(state, *others):
    rows = state[0].shape[0]
    return pl.pallas_call(
        merge_kernel,
        out_shape=jax.ShapeDtypeStruct((rows, HEAD), jnp.bfloat16),
        in_specs=[VMEM] * (2 + len(others)),
        out_specs=ANY,
        scratch_shapes=[
            pltpu.VMEM((rows, HEAD), jnp.bfloat16),
            pltpu.SemaphoreType.DMA((rows // BLOCK,)),
        ],
        cost_estimate=cost(8 * rows * HEAD, 10 * rows * HEAD),
        compiler_params=grant(4),
        name="merge",
    )(*state, *others)


def shards(queries, keys, values, allowed):
    rows = queries.shape[0]
    own = rows // BLOCK
    spots = lax.axis_size("blk")
    levels = spots // 2

    def hop(value, target):
        pairs = []
        for i in range(spots):
            high, side = target(i // 2, i % 2)
            if 0 <= high < levels:
                pairs.append((i, high * 2 + side))
        return lax.ppermute(value, "blk", pairs)

    def across(value):
        return hop(value, lambda high, side: (high, 1 - side))

    def swap(value):
        return lax.ppermute(value, "node", [(0, 1), (1, 0)])

    def trade(value, turn):
        pairs = []
        for i in range(spots):
            high, side = i // 2, i % 2
            for core in range(2):
                far = (high ^ 1) if core == turn else ((high + 1) ^ 1) - 1
                if 0 <= far < levels:
                    pairs.append((2 * i + core, 2 * (far * 2 + side) + core))
        return lax.ppermute(value, ("blk", "node"), pairs)

    def visit(value):
        pairs = []
        for i in range(spots):
            high, side = i // 2, i % 2
            for core in range(2):
                came = side if core == 0 else 1 - side
                far = high + 1 - 2 * came
                if 0 < far < levels - 1:
                    pairs.append((2 * i + core, 2 * (far * 2 + came) + core))
        return lax.ppermute(value, ("blk", "node"), pairs)

    tie = lax.optimization_barrier
    bundled, turned = bundle(queries, keys, values)
    mates = across(turned)
    first = trade(bundled, 0)
    second = trade(bundled, 1)
    other = swap(bundled)
    table = lists(allowed, own, spots)
    *near, sums, stats = attend(0, table, turned, (bundled, other))
    mate_state = attend(1, table, mates, gathered=near)
    parcel = choose(mates, turned)
    first, second, mates, mate_state = tie((first, second, mates, mate_state))
    guests = visit(parcel)
    beside = (first, swap(first), second, swap(second))
    mate_part, *beside, _, _ = attend(2, table, mates, beside, state=mate_state, pack=True, spare=2)
    one = across(mate_part)
    state = attend(3, table, turned, gathered=beside, state=(sums, stats))
    (guest_part,) = attend(4, table, guests, gathered=beside, pack=True)
    homeward = []
    for i in range(2, spots - 2):
        high, side = i // 2, i % 2
        homeward.append((i, (high - 1 + 2 * side) * 2 + 1 - side))
    two = lax.ppermute(guest_part, "blk", homeward)
    return merge(state, one, two)


def solution(mesh):
    placed = (
        P(("grp", "blk", "node"), None),
        P(("grp", "blk", "node"), None),
        P(("grp", "blk", "node"), None),
        P("grp", None),
    )
    return jax.shard_map(
        shards,
        mesh=mesh,
        in_specs=placed,
        out_specs=P(("grp", "blk", "node"), None),
        check_vma=False,
    )
```
